32 devices in a mesh: pair: 8 (over z, y), aux: 4 (over x, core).
Axes of the slice: x: 2, y: 2, z: 4, core: 2. Of those that a mesh axis runs over, the one named last changes fastest.
Arguments:
- pair_factors: bfloat16 [16384, 16384], P('pair', 'aux'), may hold values from -0.077339804 to 0.077339804
- pair_weights: float32 [16384], P('pair'), may hold values from 0.08 to 0.8
- probes: float32 [16384, 64], P('aux'), may hold values from -12 to 12
Outputs:
- last_vectors: float32 [16384, 64], P('aux', 'pair')
- moments: float32 [9], replicated
- energy: float32 [1], replicated
The draws below stay inside these ranges and needn't reach their ends.
All inputs are finite; a program needn't handle non-finite values.
Results may differ from the reference program's by a relative error of at most 0.019.
Values may be sent and summed in bfloat16 or wider, within the bound.
No kernel may reach another device: no remote copies, remote signals or barrier semaphores. Data moves between devices by JAX's collectives and lax.ppermute only.
A program may use at most 64 MiB of HBM per device.

```python
import math
import jax
import jax.numpy as jnp
import numpy as np
from jax import lax

AUXDIM = 16384
NPROBE = 64
ITERS = 8
PAIRS = 16384


def draw_pair_factors(key, part):
    scale = 1.0 / jnp.sqrt(jnp.float32(PAIRS + AUXDIM))
    scale_key = jax.random.fold_in(key, 7)
    base_key = jax.random.fold_in(key, 11)
    log_square = jax.random.uniform(scale_key, (AUXDIM,), jnp.float32, jnp.log(0.3), jnp.log(12.0))
    column_norm = jnp.exp(0.5 * log_square)
    base = jax.random.truncated_normal(base_key, -4.0, 4.0, (PAIRS, AUXDIM), jnp.float32)
    return (base * column_norm[None, :] * scale).astype(jnp.bfloat16)


def draw_probes(key, part):
    column = jnp.arange(NPROBE, dtype=jnp.float32) / (NPROBE - 1)
    base = jax.random.truncated_normal(key, -4.0, 4.0, (AUXDIM, NPROBE), jnp.float32)
    scale = jnp.exp(column * 0.5 * jnp.log(9.0))
    return base * scale[None, :]


def shard_levels(stream_key, extent, cuts, least, top_value):
    gain = 1.0
    for axis_at, parts in cuts:
        heights = jax.random.uniform(jax.random.fold_in(jax.random.fold_in(stream_key, 6), axis_at), (parts,), jnp.float32, least / len(cuts), top_value / len(cuts))
        gain = gain * jnp.repeat(jnp.exp(heights), extent[axis_at] // parts).reshape((-1,) + (1,) * (len(extent) - 1 - axis_at))
    return gain


def setup_inputs(seed: int = 0) -> dict:
    key_of = jax.random.split(jax.random.key(seed), 4)
    return {
        "pair_factors": draw_pair_factors(jax.random.fold_in(key_of[3], 71), 0),
        "pair_weights": jnp.clip(jnp.exp(math.log(0.8) - 2.3025851 * jax.random.uniform(key_of[1], (PAIRS,), jnp.float32) ** shard_levels(key_of[1], (PAIRS,), ((0, 8),), -0.2, 0.2)), 0.08, 0.8),
        "probes": draw_probes(jax.random.fold_in(key_of[3], 71), 0),
    }


spread = 5.0


def cheb_coefficients(order_count):
    node_count = 64
    angles = (np.arange(node_count) + 0.5) * np.pi / node_count
    samples = np.log(1.0 + spread * (np.cos(angles) + 1.0) / 2.0)
    values = [2.0 / node_count * np.sum(samples * np.cos(degree * angles)) for degree in range(order_count)]
    values[0] = values[0] / 2.0
    return np.array(values)


def reference(pair_factors, pair_weights, probes):
    divisor = NPROBE * AUXDIM
    previous = probes
    current = probes
    moment_list = [jnp.sum(probes * current) / divisor]
    for degree in range(ITERS):
        rows = jnp.dot(pair_factors, current.astype(jnp.bfloat16), preferred_element_type=jnp.float32)
        scaled = (pair_weights[:, None] * rows).astype(jnp.bfloat16)
        image = lax.dot_general(pair_factors, scaled, (((0,), (0,)), ((), ())), preferred_element_type=jnp.float32)
        mapped = (2.0 / spread) * image - current
        following = mapped if degree == 0 else 2.0 * mapped - previous
        previous, current = current, following
        moment_list.append(jnp.sum(probes * current) / divisor)
    moments = jnp.stack(moment_list).astype(jnp.float32)
    coefficients = jnp.asarray(cheb_coefficients(ITERS + 1)).astype(moments.dtype)
    energy = jnp.sum(coefficients * moments).reshape(1)
    return current, moments, energy
```

```python
import functools

import jax
import jax.numpy as jnp
import numpy as np
from jax import lax
from jax.experimental import pallas as pl
from jax.experimental.pallas import tpu as pltpu
from jax.sharding import PartitionSpec as P

ITERS = 8


spread = 5.0


BF = jnp.bfloat16
F32 = jnp.float32
VM = pl.BlockSpec(memory_space=pltpu.VMEM)
SM = pl.BlockSpec(memory_space=pltpu.SMEM)
NT = (((1,), (1,)), ((), ()))
TILE = 512


def cheb_coefficients(order_count):
    node_count = 64
    angles = (np.arange(node_count) + 0.5) * np.pi / node_count
    samples = np.log(1.0 + spread * (np.cos(angles) + 1.0) / 2.0)
    values = [
        2.0 / node_count * np.sum(samples * np.cos(degree * angles))
        for degree in range(order_count)
    ]
    values[0] = values[0] / 2.0
    return np.array(values)


def call(body, name, outs, specs, args, flops=0, scratch=(), limit=8):
    moved = sum(a.size * a.dtype.itemsize for a in args)
    return pl.pallas_call(
        body,
        out_shape=outs,
        in_specs=specs,
        out_specs=jax.tree.map(lambda _: VM, outs),
        scratch_shapes=scratch,
        compiler_params=pltpu.CompilerParams(vmem_limit_bytes=limit << 20),
        cost_estimate=pl.CostEstimate(flops=flops, bytes_accessed=moved, transcendentals=0),
        name=name,
    )(*args)


def hold_body(b, o, sem):
    copy = pltpu.make_async_copy(b, o, sem)
    copy.start()
    copy.wait()


def hold(b):
    return pl.pallas_call(
        hold_body,
        out_shape=pltpu.VMEM(b.shape, b.dtype),
        in_specs=[pl.BlockSpec(memory_space=pltpu.HBM)],
        out_specs=VM,
        scratch_shapes=[pltpu.SemaphoreType.DMA],
        compiler_params=pltpu.CompilerParams(vmem_limit_bytes=4 << 20),
        name="hold",
    )(b)


def struct(shape, dtype):
    return jax.ShapeDtypeStruct(shape, dtype)


def swap(x, axis, bit):
    size = lax.axis_size(axis)
    return lax.ppermute(x, axis, [(i, i ^ bit) for i in range(size)])


def rows_body(sel, b, v, o):
    half = o.shape[1]
    blocks, _, sub = v.shape
    tile = min(TILE, half)
    for n in range(0, half, tile):
        at = pl.ds(pl.multiple_of(sel[0] * half + n, tile), tile)
        acc = None
        for p in range(blocks):
            part = lax.dot_general(
                v[p], b[at, p * sub : (p + 1) * sub], NT, preferred_element_type=F32
            )
            acc = part if acc is None else acc + part
        o[:, n : n + tile] = acc.astype(o.dtype)


def add_body(keep, got, total, sent):
    t = keep[...] + got[...].astype(F32)
    total[...] = t
    sent[...] = t.astype(BF)


def scale_body(total, got, w, o):
    o[...] = (w[...] * (total[...] + got[...].astype(F32))).astype(BF)


def image_first_body(sel, b, s, o):
    half = s.shape[1]
    at = pl.ds(pl.multiple_of(sel[0] * half, half), half)
    for n in range(0, o.shape[1], TILE):
        o[:, n : n + TILE] = jnp.dot(
            s[...], b[at, n : n + TILE], preferred_element_type=F32
        )


def image_second_body(sel, b, s, first, o):
    half = s.shape[1]
    at = pl.ds(pl.multiple_of(sel[0] * half, half), half)
    blocks, _, sub = o.shape
    for p in range(blocks):
        cols = slice(p * sub, (p + 1) * sub)
        part = jnp.dot(s[...], b[at, cols], preferred_element_type=F32)
        o[p] = (first[:, cols] + part).astype(BF)


def image_last_body(sel, b, s, first, cur, prev, o, whole):
    half = s.shape[1]
    at = pl.ds(pl.multiple_of(sel[0] * half, half), half)
    blocks, cols_each, width = o.shape
    sub = cur.shape[1]
    for n in range(0, width, TILE):
        cols = slice(n, n + TILE)
        part = jnp.dot(s[...], b[at, cols], preferred_element_type=F32)
        whole[:, cols] = (4.0 / spread) * (first[:, cols] + part)
    own = pl.ds(pl.multiple_of(sel[1] * sub, sub), sub)
    whole[:, own] = whole[:, own] - 2.0 * cur[...] - prev[...]
    for p in range(blocks):
        o[p] = whole[p * cols_each : (p + 1) * cols_each, :].astype(BF)


def lane_sums(x):
    rows = jnp.sum(x, axis=0, keepdims=True)
    out = rows[:, :128]
    for n in range(128, rows.shape[1], 128):
        out = out + rows[:, n : n + 128]
    return out


def recur_body(degree, got, cur, prev, z, sums_in, new, sent, sums):
    image = got[0].astype(F32)
    for p in range(1, got.shape[0]):
        image = image + got[p].astype(F32)
    mapped = (2.0 / spread) * image - cur[...]
    value = mapped if degree == 0 else 2.0 * mapped - prev[...]
    new[...] = value
    for p in range(sent.shape[0]):
        sent[p] = value.astype(BF)
    sums[...] = sums_in[...]
    order = degree + 1
    if order == 1:
        sums[0:1] = lane_sums(z[...] * z[...])
    if order <= 4:
        sums[order : order + 1] = lane_sums(z[...] * value)
    if order in (3, 4):
        sums[2 * order - 1 : 2 * order] = lane_sums(value * cur[...])
        sums[2 * order : 2 * order + 1] = lane_sums(value * value)


def last_body(got, o):
    total = got[0].astype(F32)
    for p in range(1, got.shape[0]):
        total = total + got[p].astype(F32)
    o[...] = total


def finish_body(divisor, coefficients, sums, after, moments, energy):
    totals = jnp.sum(sums[...], axis=1, keepdims=True) / divisor
    lane = lax.broadcasted_iota(jnp.int32, moments.shape, 1)
    row = jnp.zeros(moments.shape, F32)
    weighed = jnp.zeros(energy.shape, F32)
    for k, coefficient in enumerate(coefficients):
        moment = totals[k : k + 1]
        if k > 4:
            moment = 2.0 * moment - totals[k % 2 : k % 2 + 1]
        row = jnp.where(lane == k, moment, row)
        weighed = weighed + float(coefficient) * moment
    moments[...] = row
    energy[...] = weighed


def per_device(pair_factors, pair_weights, probes):
    aux_size, pair_size = lax.axis_size("aux"), lax.axis_size("pair")
    pairs, width = pair_factors.shape
    count = probes.shape[1]
    half, sub = pairs // 2, width // pair_size
    flops = 2 * pairs * width * count
    core = lax.axis_index("aux") % 2
    place = lax.axis_index("pair")
    mine = jnp.stack([core, place]).astype(jnp.int32)
    other = jnp.stack([1 - core, place]).astype(jnp.int32)

    wide = probes.T
    z = lax.dynamic_slice_in_dim(wide, place * sub, sub, 1)
    weights = lax.dynamic_slice_in_dim(pair_weights, core * half, half)[None, :]
    gathered = wide.astype(BF).reshape(count, pair_size, sub).transpose(1, 0, 2)
    sums = jnp.zeros((16, 128), F32)
    z, weights, gathered, mine, other, sums, pair_factors = lax.optimization_barrier(
        (z, weights, gathered, mine, other, sums, pair_factors)
    )
    pair_factors = hold(pair_factors)
    previous = current = z

    half_f32 = struct((count, half), F32)
    half_bf = struct((count, half), BF)
    for degree in range(ITERS):
        give = call(
            rows_body, "rows_give", half_bf, [SM, VM, VM], (other, pair_factors, gathered), flops // 2
        )
        take = swap(give, "aux", 1)
        total = call(
            rows_body, "rows_keep", half_f32, [SM, VM, VM], (mine, pair_factors, gathered), flops // 2
        )
        bit = 2
        while bit < aux_size:
            total, sent = call(add_body, "add", (half_f32, half_bf), [VM] * 2, (total, take))
            take = swap(sent, "aux", bit)
            bit *= 2
        scaled = call(scale_body, "scale", half_bf, [VM] * 3, (total, take, weights))
        scaled_other = swap(scaled, "aux", 1)
        first = call(
            image_first_body,
            "image_first",
            struct((count, width), F32),
            [SM, VM, VM],
            (mine, pair_factors, scaled),
            flops // 2,
        )
        if degree == ITERS - 1:
            image = call(
                image_last_body,
                "image_last",
                struct((pair_size, count // pair_size, width), BF),
                [SM] + [VM] * 5,
                (other, pair_factors, scaled_other, first, current, previous),
                flops // 2,
                [pltpu.VMEM((count, width), F32)],
            )
            got = lax.all_to_all(image, "pair", split_axis=0, concat_axis=0)
            last = call(last_body, "last", struct((count // pair_size, width), F32), [VM], (got,))
            break
        image = call(
            image_second_body,
            "image_second",
            struct((pair_size, count, sub), BF),
            [SM] + [VM] * 3,
            (other, pair_factors, scaled_other, first),
            flops // 2,
        )
        got = lax.all_to_all(image, "pair", split_axis=0, concat_axis=0)
        following, sent, sums = call(
            functools.partial(recur_body, degree),
            "recur",
            (struct((count, sub), F32), struct((pair_size, count, sub), BF), struct((16, 128), F32)),
            [VM] * 5,
            (got, current, previous, z, sums),
        )
        gathered = lax.all_to_all(sent, "pair", split_axis=0, concat_axis=0)
        previous, current = current, following
        if degree == 3:
            for axis, size in (("aux", aux_size), ("pair", pair_size)):
                bit = 1
                while bit < size:
                    sums = sums + swap(sums, axis, bit)
                    bit *= 2

    divisor = count * width * aux_size
    moments, energy = call(
        functools.partial(finish_body, divisor, cheb_coefficients(ITERS + 1)),
        "finish",
        (struct((1, ITERS + 1), F32), struct((1, 1), F32)),
        [VM] * 2,
        (sums, got),
    )
    moments, energy = moments.reshape(ITERS + 1), energy.reshape(1)
    return (last.T, moments, energy)


def solution(mesh):
    placed = (P("pair", "aux"), P("pair"), P("aux", None))
    return jax.shard_map(
        per_device,
        mesh=mesh,
        in_specs=placed,
        out_specs=(P("aux", "pair"), P(), P()),
        check_vma=False,
    )
```

```python
import functools

import jax
import jax.numpy as jnp
import numpy as np
from jax import lax
from jax.experimental import pallas as pl
from jax.experimental.pallas import tpu as pltpu
from jax.sharding import PartitionSpec as P

ITERS = 8


spread = 5.0


BF = jnp.bfloat16
F32 = jnp.float32
VM = pl.BlockSpec(memory_space=pltpu.VMEM)
NT = (((1,), (1,)), ((), ()))
TILE = 512


def cheb_coefficients(order_count):
    node_count = 64
    angles = (np.arange(node_count) + 0.5) * np.pi / node_count
    samples = np.log(1.0 + spread * (np.cos(angles) + 1.0) / 2.0)
    values = [
        2.0 / node_count * np.sum(samples * np.cos(degree * angles))
        for degree in range(order_count)
    ]
    values[0] = values[0] / 2.0
    return np.array(values)


def call(body, name, outs, args, flops=0, scratch=(), limit=8, specs=None):
    moved = sum(a.size * a.dtype.itemsize for a in args)
    return pl.pallas_call(
        body,
        out_shape=outs,
        in_specs=specs or [VM] * len(args),
        out_specs=jax.tree.map(lambda _: VM, outs),
        scratch_shapes=scratch,
        compiler_params=pltpu.CompilerParams(vmem_limit_bytes=limit << 20),
        cost_estimate=pl.CostEstimate(flops=flops, bytes_accessed=moved, transcendentals=0),
        name=name,
    )(*args)


def struct(shape, dtype):
    return jax.ShapeDtypeStruct(shape, dtype)


def swap(x, axis, bit):
    size = lax.axis_size(axis)
    return lax.ppermute(x, axis, [(i, i ^ bit) for i in range(size)])


def bit_of(axis, bit):
    return lax.rem(lax.div(lax.axis_index(axis), jnp.int32(bit)), jnp.int32(2))


def span(start, size):
    return pl.ds(pl.multiple_of(start, size), size)


def start_body(b, v, held, give, keep, sems):
    pairs = b.shape[0]
    half = pairs // 2
    core = bit_of("aux", 1)
    copies = []
    for k in range(pairs // TILE):
        part = (1 - core) if k * TILE < half else core
        at = span(part * half + (k * TILE) % half, TILE)
        copies.append((pltpu.make_async_copy(b.at[at], held.at[at], sems.at[k]), at))
        copies[-1][0].start()
    for k, (copy, at) in enumerate(copies):
        copy.wait()
        out = give if k * TILE < half else keep
        cols = pl.ds((k * TILE) % half, TILE)
        acc = lax.dot_general(v[...], held[at, :], NT, preferred_element_type=F32)
        out[:, cols] = acc.astype(out.dtype)


def rows_part(b, own, far, region, pairs_at, acc):
    base, bit = region
    width = own.shape[1]
    mine = bit_of("pair", bit)
    near_at = span(base + mine * width, width)
    far_at = span(base + (1 - mine) * width, width)
    part = lax.dot_general(own[...], b[pairs_at, near_at], NT, preferred_element_type=F32)
    acc = part if acc is None else acc + part
    return acc + lax.dot_general(far[...], b[pairs_at, far_at], NT, preferred_element_type=F32)


def rows_first_body(region, b, own, far, o):
    tile = min(TILE, o.shape[1])
    for n in range(0, o.shape[1], tile):
        o[:, n : n + tile] = rows_part(b, own, far, region, pl.ds(n, tile), None)


def rows_second_body(region, keep, offset, b, own, far, first, o):
    half = b.shape[0] // 2
    tile = min(TILE, o.shape[1])
    core = bit_of("aux", 1)
    part = core if keep else 1 - core
    for n in range(0, o.shape[1], tile):
        at = span(part * half + offset + n, tile)
        acc = rows_part(b, own, far, region, at, first[:, at])
        o[:, n : n + tile] = acc.astype(o.dtype)


def add_body(offset, keep, got, total, sent):
    t = keep[...] + got[:, offset : offset + keep.shape[1]].astype(F32)
    total[...] = t
    sent[...] = t.astype(BF)


def scale_body(offset, total, got, w, o):
    weights = w[:, offset : offset + o.shape[1]]
    o[...] = (weights * (total[...] + got[...].astype(F32))).astype(BF)


def image_dot(b, own, far, offset, cols):
    half, size = b.shape[0] // 2, own.shape[1]
    core = bit_of("aux", 1)
    near_at = span(core * half + offset, size)
    far_at = span((1 - core) * half + offset, size)
    near = jnp.dot(own[...], b[near_at, cols], preferred_element_type=F32)
    return near + jnp.dot(far[...], b[far_at, cols], preferred_element_type=F32)


def image_first_body(offset, b, own, far, o):
    for n in range(0, o.shape[1], TILE):
        cols = pl.ds(n, TILE)
        o[:, cols] = image_dot(b, own, far, offset, cols)


def image_second_body(region, keep, offset, b, own, far, first, o):
    base, bit = region
    width = o.shape[1]
    tile = min(TILE, width)
    mine = bit_of("pair", bit)
    part = mine if keep else 1 - mine
    for n in range(0, width, tile):
        cols = span(base + part * width + n, tile)
        acc = first[:, cols] + image_dot(b, own, far, offset, cols)
        o[:, n : n + tile] = acc.astype(o.dtype)


def split_body(bit, keep, got, sent, kept):
    width = kept.shape[1]
    mine = bit_of("pair", bit)
    stay, leave = span(mine * width, width), span((1 - mine) * width, width)
    sent[...] = (keep[:, leave] + got[:, leave].astype(F32)).astype(BF)
    kept[...] = keep[:, stay] + got[:, stay].astype(F32)


def sum_body(keep, got, sent):
    sent[...] = (keep[...].astype(F32) + got[...].astype(F32)).astype(BF)


def pack_body(bit, own, far, o):
    width = own.shape[1]
    mine = bit_of("pair", bit)
    o[:, span(mine * width, width)] = own[...]
    o[:, span((1 - mine) * width, width)] = far[...]


def shard_start(base, bits, width):
    start = base
    for bit in bits:
        width //= 2
        start = start + bit_of("pair", bit) * width
    return start


def image_last_body(chunks, copies, offset, b, own, far, first, *refs):
    state, (o, whole) = refs[:-2], refs[-2:]
    blocks, cols_each, width = o.shape
    for n in range(0, width, TILE):
        cols = pl.ds(n, TILE)
        acc = first[:, cols] + image_dot(b, own, far, offset, cols)
        whole[:, cols] = (4.0 / spread) * acc
    for chunk, (base, bits, _) in enumerate(chunks):
        cur, prev = state[2 * chunk : 2 * chunk + 2]
        start = shard_start(base, bits, width // len(chunks))
        cols = span(start, cur.shape[1])
        whole[:, cols] = whole[:, cols] - (2.0 / copies) * cur[...] - (1.0 / copies) * prev[...]
    for p in range(blocks):
        o[p] = whole[p * cols_each : (p + 1) * cols_each, :].astype(BF)


def lane_sums(x):
    rows = jnp.sum(x, axis=0, keepdims=True)
    out = rows[:, :128]
    for n in range(128, rows.shape[1], 128):
        out = out + rows[:, n : n + 128]
    return out


def recur_body(degree, mine, got, cur, prev, z, sums_in, new, sent, sums):
    image = mine[...].astype(F32) + got[...].astype(F32)
    mapped = (2.0 / spread) * image - cur[...]
    value = mapped if degree == 0 else 2.0 * mapped - prev[...]
    new[...] = value
    sent[...] = value.astype(BF)
    sums[...] = sums_in[...]
    order = degree + 1
    if order == 1:
        sums[0:1] += lane_sums(z[...] * z[...])
    if order <= 4:
        sums[order : order + 1] += lane_sums(z[...] * value)
    if order in (3, 4):
        sums[2 * order - 1 : 2 * order] += lane_sums(value * cur[...])
        sums[2 * order : 2 * order + 1] += lane_sums(value * value)


def last_body(got, o):
    total = got[0].astype(F32)
    for p in range(1, got.shape[0]):
        total = total + got[p].astype(F32)
    o[...] = total


def finish_body(divisor, coefficients, sums, after, moments, energy):
    totals = jnp.sum(sums[...], axis=1, keepdims=True) / divisor
    lane = lax.broadcasted_iota(jnp.int32, moments.shape, 1)
    row = jnp.zeros(moments.shape, F32)
    weighed = jnp.zeros(energy.shape, F32)
    for k, coefficient in enumerate(coefficients):
        moment = totals[k : k + 1]
        if k > 4:
            moment = 2.0 * moment - totals[k % 2 : k % 2 + 1]
        row = jnp.where(lane == k, moment, row)
        weighed = weighed + float(coefficient) * moment
    moments[...] = row
    energy[...] = weighed


def per_device(pair_factors, pair_weights, probes):
    aux_size, pair_size = lax.axis_size("aux"), lax.axis_size("pair")
    pairs, width = pair_factors.shape
    count = probes.shape[1]
    half, quarter = pairs // 2, pairs // 4
    flops = 2 * pairs * width * count
    part = functools.partial

    order = [1 << k for k in range(pair_size.bit_length() - 1)]
    top, lower = order[-1], order[:-1]
    chunk_width = width // 2
    chunks = [
        (0, lower[::-1], [top]),
        (chunk_width, lower, [top]),
    ]
    copies = 2
    shard = chunk_width * copies // pair_size

    wide = probes.T
    z = [
        lax.dynamic_slice_in_dim(wide, shard_start(base, bits, chunk_width), shard, 1)
        for base, bits, _ in chunks
    ]
    core = bit_of("aux", 1)
    weights = lax.dynamic_slice_in_dim(pair_weights, core * half, half)[None, :]
    vectors = wide.astype(BF)
    sums = jnp.zeros((16, 128), F32)
    z, weights, vectors, sums, pair_factors = lax.optimization_barrier(
        (z, weights, vectors, sums, pair_factors)
    )
    previous, current = list(z), list(z)

    for degree in range(ITERS):
        if degree == 0:
            pair_factors, give, keep = call(
                start_body,
                "start",
                (
                    pltpu.VMEM(pair_factors.shape, BF),
                    struct((count, half), BF),
                    struct((count, half), F32),
                ),
                (pair_factors, vectors),
                flops,
                [pltpu.SemaphoreType.DMA((pairs // TILE,))],
                34,
                [pl.BlockSpec(memory_space=pltpu.HBM), VM],
            )
            take = swap(give, "aux", 1)
            kept = [keep[:, :quarter], keep[:, quarter:]]
        else:
            regions = [(base, (bits + full)[0]) for base, bits, full in chunks]
            first = call(
                part(rows_first_body, regions[0]),
                "rows_first",
                struct((count, pairs), F32),
                (pair_factors, *gathered[0]),
                flops // 2,
            )
            args = (pair_factors, *gathered[1], first)
            body = part(rows_second_body, regions[1])
            give = call(
                part(body, False, 0), "rows_give", struct((count, half), BF), args, flops // 4
            )
            take = swap(give, "aux", 1)
            kept = [
                call(
                    part(body, True, offset),
                    "rows_keep",
                    struct((count, quarter), F32),
                    args,
                    flops // 8,
                )
                for offset in (0, quarter)
            ]
        quarters = []
        for offset, total in zip((0, quarter), kept):
            outs = (struct((count, quarter), F32), struct((count, quarter), BF))
            total, sent = call(part(add_body, offset), "add", outs, (total, take))
            bit = 2
            got = swap(sent, "aux", bit)
            while 2 * bit < aux_size:
                bit *= 2
                total, sent = call(part(add_body, 0), "add", outs, (total, got))
                got = swap(sent, "aux", bit)
            quarters.append((offset, total, got))
        scaled = []
        for offset, total, got in quarters:
            own = call(
                part(scale_body, offset), "scale", struct((count, quarter), BF), (total, got, weights)
            )
            scaled.append((own, swap(own, "aux", 1)))
        first = call(
            part(image_first_body, 0),
            "image_first",
            struct((count, width), F32),
            (pair_factors, *scaled[0]),
            flops // 2,
        )
        args = (pair_factors, *scaled[1], first)
        if degree == ITERS - 1:
            state = [x for pair in zip(current, previous) for x in pair]
            image = call(
                part(image_last_body, chunks, copies, quarter),
                "image_last",
                struct((pair_size, count // pair_size, width), BF),
                (*args, *state),
                flops // 2,
                [pltpu.VMEM((count, width), F32)],
            )
            got = lax.all_to_all(image, "pair", split_axis=0, concat_axis=0)
            last = call(last_body, "last", struct((count // pair_size, width), F32), (got,))
            break

        piece = chunk_width // 2
        work = []
        for base, bits, full in chunks:
            body = part(image_second_body, (base, bits[0]))
            sent = call(
                part(body, False, quarter), "image_give", struct((count, piece), BF), args, flops // 8
            )
            got = swap(sent, "pair", bits[0])
            work.append((sent, got))
        for at, (base, bits, full) in enumerate(chunks):
            body = part(image_second_body, (base, bits[0]))
            kept = call(
                part(body, True, quarter), "image_keep", struct((count, piece), F32), args, flops // 8
            )
            work[at] = (kept, work[at][1])
        for level in range(1, pair_size.bit_length() - 1):
            for at, (base, bits, full) in enumerate(chunks):
                if level < len(bits):
                    size = chunk_width >> (level + 1)
                    sent, kept = call(
                        part(split_body, bits[level]),
                        "split",
                        (struct((count, size), BF), struct((count, size), F32)),
                        work[at],
                    )
                    work[at] = (kept, swap(sent, "pair", bits[level]))
                else:
                    sent = call(sum_body, "sum", struct((count, shard), BF), work[at])
                    work[at] = (sent, swap(sent, "pair", full[level - len(bits)]))
        for at, (base, bits, full) in enumerate(chunks):
            following, sent, sums = call(
                part(recur_body, degree),
                "recur",
                (struct((count, shard), F32), struct((count, shard), BF), struct((16, 128), F32)),
                (*work[at], current[at], previous[at], z[at], sums),
            )
            previous[at], current[at] = current[at], following
            work[at] = (sent, swap(sent, "pair", bits[-1]))
        for level in range(len(chunks[0][1]) - 2, -1, -1):
            for at, (base, bits, full) in enumerate(chunks):
                own, far = work[at]
                packed = call(
                    part(pack_body, bits[level + 1]),
                    "pack",
                    struct((count, 2 * own.shape[1]), BF),
                    (own, far),
                )
                work[at] = (packed, swap(packed, "pair", bits[level]))
        gathered = work
        if degree == 3:
            for axis, size in (("aux", aux_size), ("pair", pair_size)):
                bit = 1
                while bit < size:
                    sums = sums + swap(sums, axis, bit)
                    bit *= 2

    divisor = count * width * aux_size * copies
    moments, energy = call(
        functools.partial(finish_body, divisor, cheb_coefficients(ITERS + 1)),
        "finish",
        (struct((1, ITERS + 1), F32), struct((1, 1), F32)),
        (sums, got),
    )
    moments, energy = moments.reshape(ITERS + 1), energy.reshape(1)
    return (last.T, moments, energy)


def solution(mesh):
    placed = (P("pair", "aux"), P("pair"), P("aux", None))
    return jax.shard_map(
        per_device,
        mesh=mesh,
        in_specs=placed,
        out_specs=(P("aux", "pair"), P(), P()),
        check_vma=False,
    )
```

```python
import functools

import jax
import jax.numpy as jnp
import numpy as np
from jax import lax
from jax.experimental import pallas as pl
from jax.experimental.pallas import tpu as pltpu
from jax.sharding import PartitionSpec as P

ITERS = 8


spread = 5.0


BF = jnp.bfloat16
F32 = jnp.float32
VM = pl.BlockSpec(memory_space=pltpu.VMEM)
TILE = 512
PIECE = 256


def cheb_coefficients(order_count):
    node_count = 64
    angles = (np.arange(node_count) + 0.5) * np.pi / node_count
    samples = np.log(1.0 + spread * (np.cos(angles) + 1.0) / 2.0)
    values = [
        2.0 / node_count * np.sum(samples * np.cos(degree * angles))
        for degree in range(order_count)
    ]
    values[0] = values[0] / 2.0
    return np.array(values)


def call(body, name, outs, args, flops=0, scratch=(), limit=8, specs=None):
    moved = sum(a.size * a.dtype.itemsize for a in args)
    return pl.pallas_call(
        body,
        out_shape=outs,
        in_specs=specs or [VM] * len(args),
        out_specs=jax.tree.map(lambda _: VM, outs),
        scratch_shapes=scratch,
        compiler_params=pltpu.CompilerParams(vmem_limit_bytes=limit << 20),
        cost_estimate=pl.CostEstimate(flops=flops, bytes_accessed=moved, transcendentals=0),
        name=name,
    )(*args)


def struct(shape, dtype):
    return jax.ShapeDtypeStruct(shape, dtype)


def swap(x, axis, bit):
    size = lax.axis_size(axis)
    return lax.ppermute(x, axis, [(i, i ^ bit) for i in range(size)])


def bit_of(axis, bit):
    return lax.rem(lax.div(lax.axis_index(axis), jnp.int32(bit)), jnp.int32(2))


def span(start, size):
    return pl.ds(pl.multiple_of(start, size), size)


def tiles(width, tile, step, unroll=1):
    def run(k, carry):
        step(pl.multiple_of(k * tile, tile))
        return carry

    lax.fori_loop(0, width // tile, run, 0, unroll=min(unroll, width // tile))


def start_body(chunks, b, wide, w, left, right, turned_left, turned_right, give, keep, more, weights, sums, *refs):
    shards, (v, sems) = refs[:-2], refs[-2:]
    sums[...] = jnp.zeros_like(sums)
    pairs, width = b.shape
    half = pairs // 2
    core = bit_of("aux", 1)

    sides = ((left, turned_left, 0), (right, turned_right, left.shape[1]))

    def copy(k, side):
        held, _, base = side
        at = span(lax.rem((1 - core) * half + k * PIECE, pairs), PIECE)
        source = b.at[at, base : base + held.shape[1]]
        return pltpu.make_async_copy(source, held.at[at], sems.at[k, 0 if base == 0 else 1]), at

    for k in range(pairs // PIECE):
        for side in sides:
            copy(k, side)[0].start()
    v[...] = wide[...].astype(BF)
    weights[...] = w[:, span(core * half, half)]
    for (base, bits, _), z in zip(chunks, shards):
        z[...] = wide[:, span(shard_start(base, bits, width // len(chunks)), z.shape[1])]

    firsts = (0, half // PIECE, (half + keep.shape[1]) // PIECE)
    for out, first in zip((give, keep, more), firsts):

        def step(n, out=out, first=first):
            k = lax.div(n, jnp.int32(PIECE))
            acc = 0.0
            for side in sides:
                move, at = copy(k + first, side)
                move.wait()
                held, turned, base = side
                for c in range(0, turned.shape[0], PIECE):
                    turned[c : c + PIECE, at] = held[at, c : c + PIECE].T
                cols = v[:, base : base + turned.shape[0]]
                acc = acc + jnp.dot(cols, turned[:, at], preferred_element_type=F32)
            out[:, pl.ds(n, PIECE)] = acc.astype(out.dtype)

        tiles(out.shape[1], PIECE, step)


def rows_part(turned, own, far, bit, pairs_at, acc):
    width = own.shape[1]
    mine = bit_of("pair", bit)
    near_at = span(mine * width, width)
    far_at = span((1 - mine) * width, width)
    part = jnp.dot(own[...], turned[near_at, pairs_at], preferred_element_type=F32)
    acc = part if acc is None else acc + part
    return acc + jnp.dot(far[...], turned[far_at, pairs_at], preferred_element_type=F32)


def rows_first_body(bit, turned, own, far, o):
    tile = min(TILE, o.shape[1])

    def step(n):
        at = pl.ds(n, tile)
        o[:, at] = rows_part(turned, own, far, bit, at, None)

    tiles(o.shape[1], tile, step)


def rows_second_body(bit, keep, offset, turned, own, far, first, o):
    half = turned.shape[1] // 2
    tile = min(TILE, o.shape[1])
    core = bit_of("aux", 1)
    part = core if keep else 1 - core

    def step(n):
        at = span(part * half + offset + n, tile)
        acc = rows_part(turned, own, far, bit, at, first[:, at])
        o[:, pl.ds(n, tile)] = acc.astype(o.dtype)

    tiles(o.shape[1], tile, step)


def add_body(offset, keep, got, total, sent):
    t = keep[...] + got[:, offset : offset + keep.shape[1]].astype(F32)
    total[...] = t
    sent[...] = t.astype(BF)


def scale_body(offset, total, got, w, o):
    weights = w[:, offset : offset + o.shape[1]]
    o[...] = (weights * (total[...] + got[...].astype(F32))).astype(BF)


def image_dot(b, own, far, offset, cols):
    half, size = b.shape[0] // 2, own.shape[1]
    core = bit_of("aux", 1)
    near_at = span(core * half + offset, size)
    far_at = span((1 - core) * half + offset, size)
    near = jnp.dot(own[...], b[near_at, cols], preferred_element_type=F32)
    return near + jnp.dot(far[...], b[far_at, cols], preferred_element_type=F32)


def image_first_body(offset, left, right, own, far, o):
    width = left.shape[1]
    for b, base in ((left, 0), (right, width)):

        def step(n, b=b, base=base):
            cols = pl.ds(n, TILE)
            o[:, pl.ds(pl.multiple_of(base + n, TILE), TILE)] = image_dot(b, own, far, offset, cols)

        tiles(width, TILE, step)


def image_second_body(region, keep, offset, b, own, far, first, o):
    base, bit = region
    width = o.shape[1]
    tile = min(TILE, width)
    mine = bit_of("pair", bit)
    part = mine if keep else 1 - mine

    def step(n):
        acc = image_dot(b, own, far, offset, span(part * width + n, tile))
        acc = first[:, span(base + part * width + n, tile)] + acc
        o[:, pl.ds(n, tile)] = acc.astype(o.dtype)

    tiles(width, tile, step, 2)


def split_body(bit, keep, got, sent, kept):
    width = kept.shape[1]
    mine = bit_of("pair", bit)
    stay, leave = span(mine * width, width), span((1 - mine) * width, width)
    sent[...] = (keep[:, leave] + got[:, leave].astype(F32)).astype(BF)
    kept[...] = keep[:, stay] + got[:, stay].astype(F32)


def sum_body(keep, got, sent):
    sent[...] = (keep[...].astype(F32) + got[...].astype(F32)).astype(BF)


def pack_body(bit, own, far, o):
    width = own.shape[1]
    mine = bit_of("pair", bit)
    o[:, span(mine * width, width)] = own[...]
    o[:, span((1 - mine) * width, width)] = far[...]


def shard_start(base, bits, width):
    start = base
    for bit in bits:
        width //= 2
        start = start + bit_of("pair", bit) * width
    return start


def image_last_body(chunks, copies, offset, left, right, own, far, first, *refs):
    state, (o, whole) = refs[:-2], refs[-2:]
    blocks, cols_each, width = o.shape
    for b, base in ((left, 0), (right, left.shape[1])):

        def step(n, b=b, base=base):
            cols = pl.ds(pl.multiple_of(base + n, TILE), TILE)
            acc = first[:, cols] + image_dot(b, own, far, offset, pl.ds(n, TILE))
            whole[:, cols] = (4.0 / spread) * acc

        tiles(left.shape[1], TILE, step)
    for chunk, (base, bits, _) in enumerate(chunks):
        cur, prev = state[2 * chunk : 2 * chunk + 2]
        start = shard_start(base, bits, width // len(chunks))
        cols = span(start, cur.shape[1])
        whole[:, cols] = whole[:, cols] - (2.0 / copies) * cur[...] - (1.0 / copies) * prev[...]
    for p in range(blocks):
        o[p] = whole[p * cols_each : (p + 1) * cols_each, :].astype(BF)


def lane_sums(x):
    rows = jnp.sum(x, axis=0, keepdims=True)
    out = rows[:, :128]
    for n in range(128, rows.shape[1], 128):
        out = out + rows[:, n : n + 128]
    return out


def recur_body(opening, push, mine, got, cur, prev, z, sums_in, new, sent, sums):
    image = mine[...].astype(F32) + got[...].astype(F32)
    mapped = (2.0 / spread) * image - cur[...]
    value = mapped if opening else 2.0 * mapped - prev[...]
    new[...] = value
    sent[...] = value.astype(BF)
    before = z[...] if opening else value
    rows = [z[...] * value, before * cur[...], value * value]
    if push:
        sums[3:] = sums_in[:-3]
    else:
        sums[...] = sums_in[...]
    for k, row in enumerate(rows):
        total = lane_sums(row)
        sums[k : k + 1] = total if push else sums_in[k : k + 1] + total


def last_body(got, o):
    total = got[0].astype(F32)
    for p in range(1, got.shape[0]):
        total = total + got[p].astype(F32)
    o[...] = total


def finish_body(divisor, coefficients, sums, after, moments, energy):
    totals = jnp.sum(sums[...], axis=1, keepdims=True) / divisor

    def total(order, k):
        row = 3 * (ITERS - 1 - order) + k
        return totals[row : row + 1]

    found = [total(1, 1)] + [total(order, 0) for order in range(1, 5)]
    found += [2.0 * total(order // 2 + order % 2, 2 - order % 2) - found[order % 2] for order in range(5, ITERS + 1)]
    lane = lax.broadcasted_iota(jnp.int32, moments.shape, 1)
    row = jnp.zeros(moments.shape, F32)
    weighed = jnp.zeros(energy.shape, F32)
    for k, coefficient in enumerate(coefficients):
        row = jnp.where(lane == k, found[k], row)
        weighed = weighed + float(coefficient) * found[k]
    moments[...] = row
    energy[...] = weighed


def per_device(pair_factors, pair_weights, probes):
    aux_size, pair_size = lax.axis_size("aux"), lax.axis_size("pair")
    pairs, width = pair_factors.shape
    count = probes.shape[1]
    half, quarter = pairs // 2, pairs // 4
    flops = 2 * pairs * width * count
    part = functools.partial

    order = [1 << k for k in range(pair_size.bit_length() - 1)]
    top, lower = order[-1], order[:-1]
    chunk_width = width // 2
    chunks = [
        (0, lower[::-1], [top]),
        (chunk_width, lower, [top]),
    ]
    copies = 2
    shard = chunk_width * copies // pair_size

    left, right, turned_left, turned_right, give, keep, more, weights, sums, *z = call(
        part(start_body, chunks),
        "start",
        (
            pltpu.VMEM((pairs, chunk_width), BF),
            pltpu.VMEM((pairs, chunk_width), BF),
            pltpu.VMEM((chunk_width, pairs), BF),
            pltpu.VMEM((chunk_width, pairs), BF),
            struct((count, half), BF),
            struct((count, quarter), F32),
            struct((count, quarter), F32),
            struct((1, half), F32),
            struct((24, 128), F32),
            *[struct((count, shard), F32) for _ in chunks],
        ),
        (pair_factors, probes.T, pair_weights[None, :]),
        flops,
        [pltpu.VMEM((count, width), BF), pltpu.SemaphoreType.DMA((pairs // PIECE, 2))],
        20,
        [pl.BlockSpec(memory_space=pltpu.HBM), VM, VM],
    )
    previous, current = list(z), list(z)
    outs = (struct((count, quarter), F32), struct((count, quarter), BF))

    def later_rows(gathered):
        first = call(
            part(rows_first_body, chunks[0][1][0]),
            "rows_first",
            struct((count, pairs), F32),
            (turned_left, *gathered[0]),
            flops // 2,
        )
        args = (turned_right, *gathered[1], first)
        body = part(rows_second_body, chunks[1][1][0])
        give = call(part(body, False, 0), "rows_give", struct((count, half), BF), args, flops // 4)
        take = swap(give, "aux", 1)
        kept = [
            call(
                part(body, True, offset), "rows_keep", struct((count, quarter), F32), args, flops // 8
            )
            for offset in (0, quarter)
        ]
        return take, kept

    def scaled_rows(take, kept):
        quarters = []
        for offset, total in zip((0, quarter), kept):
            total, sent = call(part(add_body, offset), "add", outs, (total, take))
            bit = 2
            got = swap(sent, "aux", bit)
            while 2 * bit < aux_size:
                bit *= 2
                total, sent = call(part(add_body, 0), "add", outs, (total, got))
                got = swap(sent, "aux", bit)
            quarters.append((offset, total, got))
        scaled = []
        for offset, total, got in quarters:
            own = call(
                part(scale_body, offset), "scale", struct((count, quarter), BF), (total, got, weights)
            )
            scaled.append((own, swap(own, "aux", 1)))
        first = call(
            part(image_first_body, 0),
            "image_first",
            struct((count, width), F32),
            (left, right, *scaled[0]),
            flops // 2,
        )
        return (*scaled[1], first)

    piece = chunk_width // 2

    def next_vectors(opening, args, current, previous, sums):
        work, following = [], []
        sides = ((left, *args), (right, *args))
        for side, (base, bits, full) in zip(sides, chunks):
            body = part(image_second_body, (base, bits[0]))
            sent = call(
                part(body, False, quarter), "image_give", struct((count, piece), BF), side, flops // 8
            )
            got = swap(sent, "pair", bits[0])
            work.append((sent, got))
        for at, (base, bits, full) in enumerate(chunks):
            body = part(image_second_body, (base, bits[0]))
            kept = call(
                part(body, True, quarter),
                "image_keep",
                struct((count, piece), F32),
                sides[at],
                flops // 8,
            )
            work[at] = (kept, work[at][1])
        for level in range(1, pair_size.bit_length() - 1):
            for at, (base, bits, full) in enumerate(chunks):
                if level < len(bits):
                    size = chunk_width >> (level + 1)
                    sent, kept = call(
                        part(split_body, bits[level]),
                        "split",
                        (struct((count, size), BF), struct((count, size), F32)),
                        work[at],
                    )
                    work[at] = (kept, swap(sent, "pair", bits[level]))
                else:
                    sent = call(sum_body, "sum", struct((count, shard), BF), work[at])
                    work[at] = (sent, swap(sent, "pair", full[level - len(bits)]))
        for at, (base, bits, full) in enumerate(chunks):
            new, sent, sums = call(
                part(recur_body, opening, at == 0),
                "recur",
                (struct((count, shard), F32), struct((count, shard), BF), struct((24, 128), F32)),
                (*work[at], current[at], previous[at], z[at], sums),
            )
            following.append(new)
            work[at] = (sent, swap(sent, "pair", bits[-1]))
        for level in range(len(chunks[0][1]) - 2, -1, -1):
            for at, (base, bits, full) in enumerate(chunks):
                own, far = work[at]
                packed = call(
                    part(pack_body, bits[level + 1]),
                    "pack",
                    struct((count, 2 * own.shape[1]), BF),
                    (own, far),
                )
                work[at] = (packed, swap(packed, "pair", bits[level]))
        return following, work, sums

    take, kept = swap(give, "aux", 1), [keep, more]
    args = scaled_rows(take, kept)
    following, gathered, sums = next_vectors(True, args, current, previous, sums)
    previous, current = current, following

    for _ in range(1, ITERS - 1):
        args = scaled_rows(*later_rows(gathered))
        following, gathered, sums = next_vectors(False, args, current, previous, sums)
        previous, current = current, following

    args = scaled_rows(*later_rows(gathered))
    state = [x for pair in zip(current, previous) for x in pair]
    image = call(
        part(image_last_body, chunks, copies, quarter),
        "image_last",
        struct((pair_size, count // pair_size, width), BF),
        (left, right, *args, *state),
        flops // 2,
        [pltpu.VMEM((count, width), F32)],
    )
    got = lax.all_to_all(image, "pair", split_axis=0, concat_axis=0)
    hops = [("aux", 1 << k) for k in range(aux_size.bit_length() - 1)]
    for axis, bit in hops + [("pair", bit) for bit in lower]:
        sums = sums + swap(sums, axis, bit)
    last = call(last_body, "last", struct((count // pair_size, width), F32), (got,))

    divisor = count * width * aux_size
    moments, energy = call(
        functools.partial(finish_body, divisor, cheb_coefficients(ITERS + 1)),
        "finish",
        (struct((1, ITERS + 1), F32), struct((1, 1), F32)),
        (sums, got),
    )
    moments, energy = moments.reshape(ITERS + 1), energy.reshape(1)
    return (last.T, moments, energy)


def solution(mesh):
    placed = (P("pair", "aux"), P("pair"), P("aux", None))
    return jax.shard_map(
        per_device,
        mesh=mesh,
        in_specs=placed,
        out_specs=(P("aux", "pair"), P(), P()),
        check_vma=False,
    )
```

```python
import functools

import jax
import jax.numpy as jnp
import numpy as np
from jax import lax
from jax.experimental import pallas as pl
from jax.experimental.pallas import tpu as pltpu
from jax.sharding import PartitionSpec as P

ITERS = 8


spread = 5.0


BF = jnp.bfloat16
F32 = jnp.float32
VM = pl.BlockSpec(memory_space=pltpu.VMEM)
TILE = 512
PIECE = 256


def cheb_coefficients(order_count):
    node_count = 64
    angles = (np.arange(node_count) + 0.5) * np.pi / node_count
    samples = np.log(1.0 + spread * (np.cos(angles) + 1.0) / 2.0)
    values = [
        2.0 / node_count * np.sum(samples * np.cos(degree * angles))
        for degree in range(order_count)
    ]
    values[0] = values[0] / 2.0
    return np.array(values)


def call(body, name, outs, args, flops=0, scratch=(), limit=8, specs=None):
    moved = sum(a.size * a.dtype.itemsize for a in args)
    return pl.pallas_call(
        body,
        out_shape=outs,
        in_specs=specs or [VM] * len(args),
        out_specs=jax.tree.map(lambda _: VM, outs),
        scratch_shapes=scratch,
        compiler_params=pltpu.CompilerParams(vmem_limit_bytes=limit << 20),
        cost_estimate=pl.CostEstimate(flops=flops, bytes_accessed=moved, transcendentals=0),
        name=name,
    )(*args)


def struct(shape, dtype):
    return jax.ShapeDtypeStruct(shape, dtype)


def swap(x, axis, bit):
    size = lax.axis_size(axis)
    return lax.ppermute(x, axis, [(i, i ^ bit) for i in range(size)])


def bit_of(axis, bit):
    return lax.rem(lax.div(lax.axis_index(axis), jnp.int32(bit)), jnp.int32(2))


def span(start, size):
    return pl.ds(pl.multiple_of(start, size), size)


def tiles(width, tile, step, unroll=1):
    def run(k, carry):
        step(pl.multiple_of(k * tile, tile))
        return carry

    lax.fori_loop(0, width // tile, run, 0, unroll=min(unroll, width // tile))


def start_body(chunks, b, wide, w, left, right, turned_left, turned_right, give, give_more, keep, keep_more, weights, sums, *refs):
    shards, (v, sems) = refs[:-2], refs[-2:]
    sums[...] = jnp.zeros_like(sums)
    pairs, width = b.shape
    half = pairs // 2
    core = bit_of("aux", 1)

    sides = ((left, turned_left, 0), (right, turned_right, left.shape[1]))

    def copy(k, side):
        held, _, base = side
        at = span(lax.rem((1 - core) * half + k * PIECE, pairs), PIECE)
        source = b.at[at, base : base + held.shape[1]]
        return pltpu.make_async_copy(source, held.at[at], sems.at[k, 0 if base == 0 else 1]), at

    for k in range(pairs // PIECE):
        for side in sides:
            copy(k, side)[0].start()
    v[...] = wide[...].astype(BF)
    weights[...] = w[:, span(core * half, half)]
    for (base, bits, _), z in zip(chunks, shards):
        z[...] = wide[:, span(shard_start(base, bits, width // len(chunks)), z.shape[1])]

    for part, out in enumerate((give, give_more, keep, keep_more)):
        first = part * out.shape[1] // PIECE

        def step(n, out=out, first=first):
            k = lax.div(n, jnp.int32(PIECE))
            acc = 0.0
            for side in sides:
                move, at = copy(k + first, side)
                move.wait()
                held, turned, base = side
                for c in range(0, turned.shape[0], PIECE):
                    turned[c : c + PIECE, at] = held[at, c : c + PIECE].T
                cols = v[:, base : base + turned.shape[0]]
                acc = acc + jnp.dot(cols, turned[:, at], preferred_element_type=F32)
            out[:, pl.ds(n, PIECE)] = acc.astype(out.dtype)

        tiles(out.shape[1], PIECE, step)


def side_of(bit, width, far):
    mine = bit_of("pair", bit)
    return span(((1 - mine) if far else mine) * width, width)


def rows_own_body(bits, left, right, own_left, own_right, o):
    tile = min(TILE, o.shape[1])
    near = [side_of(bit, own.shape[1], False) for bit, own in zip(bits, (own_left, own_right))]

    def step(n):
        at = pl.ds(n, tile)
        acc = jnp.dot(own_left[...], left[near[0], at], preferred_element_type=F32)
        o[:, at] = acc + jnp.dot(own_right[...], right[near[1], at], preferred_element_type=F32)

    tiles(o.shape[1], tile, step)


def rows_far_body(bit, turned, far, before, o):
    tile = min(TILE, o.shape[1])
    side = side_of(bit, far.shape[1], True)

    def step(n):
        at = pl.ds(n, tile)
        o[:, at] = before[:, at] + jnp.dot(far[...], turned[side, at], preferred_element_type=F32)

    tiles(o.shape[1], tile, step)


def rows_end_body(bit, keep, offset, turned, far, before, o):
    half = turned.shape[1] // 2
    core = bit_of("aux", 1)
    at = span((core if keep else 1 - core) * half + offset, o.shape[1])
    side = side_of(bit, far.shape[1], True)
    acc = before[:, at] + jnp.dot(far[...], turned[side, at], preferred_element_type=F32)
    o[...] = acc.astype(o.dtype)


def add_body(keep, got, total, sent):
    t = keep[...] + got[...].astype(F32)
    total[...] = t
    sent[...] = t.astype(BF)


def scale_body(offset, total, got, w, *refs):
    o = refs[-1]
    weights = w[:, offset : offset + o.shape[1]]
    o[...] = (weights * (total[...] + got[...].astype(F32))).astype(BF)


def image_dot(b, own, far, offset, cols):
    half, size = b.shape[0] // 2, own.shape[1]
    core = bit_of("aux", 1)
    near_at = span(core * half + offset, size)
    far_at = span((1 - core) * half + offset, size)
    near = jnp.dot(own[...], b[near_at, cols], preferred_element_type=F32)
    return near + jnp.dot(far[...], b[far_at, cols], preferred_element_type=F32)


def image_first_body(offset, left, right, own, o):
    width = left.shape[1]
    at = span(bit_of("aux", 1) * (left.shape[0] // 2) + offset, own.shape[1])
    for b, base in ((left, 0), (right, width)):

        def step(n, b=b, base=base):
            acc = jnp.dot(own[...], b[at, pl.ds(n, TILE)], preferred_element_type=F32)
            o[:, pl.ds(pl.multiple_of(base + n, TILE), TILE)] = acc

        tiles(width, TILE, step)


def image_far_body(offset, left, right, far, before, o):
    width = left.shape[1]
    at = span((1 - bit_of("aux", 1)) * (left.shape[0] // 2) + offset, far.shape[1])
    for b, base in ((left, 0), (right, width)):

        def step(n, b=b, base=base):
            cols = pl.ds(pl.multiple_of(base + n, TILE), TILE)
            acc = jnp.dot(far[...], b[at, pl.ds(n, TILE)], preferred_element_type=F32)
            o[:, cols] = before[:, cols] + acc

        tiles(width, TILE, step, 2)


def image_second_body(region, keep, offset, b, own, far, first, o):
    base, bit = region
    width = o.shape[1]
    tile = min(TILE, width)
    mine = bit_of("pair", bit)
    part = mine if keep else 1 - mine

    def step(n):
        acc = image_dot(b, own, far, offset, span(part * width + n, tile))
        acc = first[:, span(base + part * width + n, tile)] + acc
        o[:, pl.ds(n, tile)] = acc.astype(o.dtype)

    tiles(width, tile, step, 1 if keep else 2)


def split_body(bit, keep, got, sent, kept):
    width = kept.shape[1]
    mine = bit_of("pair", bit)
    stay, leave = span(mine * width, width), span((1 - mine) * width, width)
    sent[...] = (keep[:, leave] + got[:, leave].astype(F32)).astype(BF)
    kept[...] = keep[:, stay] + got[:, stay].astype(F32)


def sum_body(keep, got, sent):
    sent[...] = (keep[...].astype(F32) + got[...].astype(F32)).astype(BF)


def pack_body(bit, own, far, o):
    width = own.shape[1]
    mine = bit_of("pair", bit)
    o[:, span(mine * width, width)] = own[...]
    o[:, span((1 - mine) * width, width)] = far[...]


def shard_start(base, bits, width):
    start = base
    for bit in bits:
        width //= 2
        start = start + bit_of("pair", bit) * width
    return start


def image_last_body(chunks, copies, offset, left, right, own, far, first, *refs):
    state, (o, whole) = refs[:-2], refs[-2:]
    blocks, cols_each, width = o.shape
    for b, base in ((left, 0), (right, left.shape[1])):

        def step(n, b=b, base=base):
            cols = pl.ds(pl.multiple_of(base + n, TILE), TILE)
            acc = first[:, cols] + image_dot(b, own, far, offset, pl.ds(n, TILE))
            whole[:, cols] = (4.0 / spread) * acc

        tiles(left.shape[1], TILE, step, 2)
    for chunk, (base, bits, _) in enumerate(chunks):
        cur, prev = state[2 * chunk : 2 * chunk + 2]
        start = shard_start(base, bits, width // len(chunks))
        cols = span(start, cur.shape[1])
        whole[:, cols] = whole[:, cols] - (2.0 / copies) * cur[...] - (1.0 / copies) * prev[...]
    for p in range(blocks):
        o[p] = whole[p * cols_each : (p + 1) * cols_each, :].astype(BF)


def lane_sums(x):
    rows = jnp.sum(x, axis=0, keepdims=True)
    out = rows[:, :128]
    for n in range(128, rows.shape[1], 128):
        out = out + rows[:, n : n + 128]
    return out


def recur_body(opening, push, mine, got, cur, prev, z, sums_in, new, sent, sums):
    image = mine[...].astype(F32) + got[...].astype(F32)
    mapped = (2.0 / spread) * image - cur[...]
    value = mapped if opening else 2.0 * mapped - prev[...]
    new[...] = value
    sent[...] = value.astype(BF)
    before = z[...] if opening else value
    rows = [z[...] * value, before * cur[...], value * value]
    if push:
        sums[3:] = sums_in[:-3]
    else:
        sums[...] = sums_in[...]
    for k, row in enumerate(rows):
        total = lane_sums(row)
        sums[k : k + 1] = total if push else sums_in[k : k + 1] + total


def last_body(got, o):
    total = got[0].astype(F32)
    for p in range(1, got.shape[0]):
        total = total + got[p].astype(F32)
    o[...] = total


def finish_body(divisor, coefficients, sums, after, moments, energy):
    totals = jnp.sum(sums[...], axis=1, keepdims=True) / divisor

    def total(order, k):
        row = 3 * (ITERS - 1 - order) + k
        return totals[row : row + 1]

    found = [total(1, 1)] + [total(order, 0) for order in range(1, 5)]
    found += [2.0 * total(order // 2 + order % 2, 2 - order % 2) - found[order % 2] for order in range(5, ITERS + 1)]
    lane = lax.broadcasted_iota(jnp.int32, moments.shape, 1)
    row = jnp.zeros(moments.shape, F32)
    weighed = jnp.zeros(energy.shape, F32)
    for k, coefficient in enumerate(coefficients):
        row = jnp.where(lane == k, found[k], row)
        weighed = weighed + float(coefficient) * found[k]
    moments[...] = row
    energy[...] = weighed


def per_device(pair_factors, pair_weights, probes):
    aux_size, pair_size = lax.axis_size("aux"), lax.axis_size("pair")
    pairs, width = pair_factors.shape
    count = probes.shape[1]
    half, quarter = pairs // 2, pairs // 4
    flops = 2 * pairs * width * count
    part = functools.partial

    order = [1 << k for k in range(pair_size.bit_length() - 1)]
    top, lower = order[-1], order[:-1]
    chunk_width = width // 2
    chunks = [
        (0, lower[::-1], [top]),
        (chunk_width, lower, [top]),
    ]
    copies = 2
    shard = chunk_width * copies // pair_size

    left, right, turned_left, turned_right, *opening, weights, sums, z_left, z_right = call(
        part(start_body, chunks),
        "start",
        (
            pltpu.VMEM((pairs, chunk_width), BF),
            pltpu.VMEM((pairs, chunk_width), BF),
            pltpu.VMEM((chunk_width, pairs), BF),
            pltpu.VMEM((chunk_width, pairs), BF),
            struct((count, quarter), BF),
            struct((count, quarter), BF),
            struct((count, quarter), F32),
            struct((count, quarter), F32),
            struct((1, half), F32),
            struct((24, 128), F32),
            *[struct((count, shard), F32) for _ in chunks],
        ),
        (pair_factors, probes.T, pair_weights[None, :]),
        flops,
        [pltpu.VMEM((count, width), BF), pltpu.SemaphoreType.DMA((pairs // PIECE, 2))],
        20,
        [pl.BlockSpec(memory_space=pltpu.HBM), VM, VM],
    )
    z = [z_left, z_right]
    previous, current = list(z), list(z)
    outs = (struct((count, quarter), F32), struct((count, quarter), BF))

    def later_rows(gathered):
        (own_left, far_left), (own_right, far_right) = gathered
        bits = [chunk[1][0] for chunk in chunks]
        whole = struct((count, pairs), F32)
        rows = call(
            part(rows_own_body, bits),
            "rows_own",
            whole,
            (turned_left, turned_right, own_left, own_right),
            flops // 2,
        )
        rows = call(
            part(rows_far_body, bits[0]), "rows_far", whole, (turned_left, far_left, rows), flops // 4
        )
        args = (turned_right, far_right, rows)
        return [
            call(
                part(rows_end_body, bits[1], keep, offset),
                "rows_keep" if keep else "rows_give",
                struct((count, quarter), F32 if keep else BF),
                args,
                flops // 16,
            )
            for keep in (False, True)
            for offset in (0, quarter)
        ]

    def scaled_rows(give, give_more, keep, keep_more):
        takes = [swap(give, "aux", 1), swap(give_more, "aux", 1)]
        quarters = []
        for offset, total, got in zip((0, quarter), (keep, keep_more), takes):
            bit = 2
            while bit < aux_size:
                total, sent = call(add_body, "add", outs, (total, got))
                got = swap(sent, "aux", bit)
                bit *= 2
            quarters.append((offset, total, got))
        whole = struct((count, width), F32)
        order, scaled = (), []
        for offset, total, got in quarters:
            own = call(
                part(scale_body, offset),
                "scale",
                struct((count, quarter), BF),
                (total, got, weights, *order),
            )
            scaled.append((own, swap(own, "aux", 1)))
            if not order:
                image = call(
                    part(image_first_body, 0), "image_first", whole, (left, right, own), flops // 4
                )
                order = (image,)
        (own, far), rest = scaled
        image = call(
            part(image_far_body, 0), "image_far", whole, (left, right, far, image), flops // 4
        )
        return (*rest, image)

    piece = chunk_width // 2

    def next_vectors(opening, args, current, previous, sums):
        work, following = [], []
        sides = ((left, *args), (right, *args))
        for side, (base, bits, full) in zip(sides, chunks):
            body = part(image_second_body, (base, bits[0]))
            sent = call(
                part(body, False, quarter), "image_give", struct((count, piece), BF), side, flops // 8
            )
            got = swap(sent, "pair", bits[0])
            work.append((sent, got))
        for at, (base, bits, full) in enumerate(chunks):
            body = part(image_second_body, (base, bits[0]))
            kept = call(
                part(body, True, quarter),
                "image_keep",
                struct((count, piece), F32),
                sides[at],
                flops // 8,
            )
            work[at] = (kept, work[at][1])
        for level in range(1, pair_size.bit_length() - 1):
            for at, (base, bits, full) in enumerate(chunks):
                if level < len(bits):
                    size = chunk_width >> (level + 1)
                    sent, kept = call(
                        part(split_body, bits[level]),
                        "split",
                        (struct((count, size), BF), struct((count, size), F32)),
                        work[at],
                    )
                    work[at] = (kept, swap(sent, "pair", bits[level]))
                else:
                    sent = call(sum_body, "sum", struct((count, shard), BF), work[at])
                    work[at] = (sent, swap(sent, "pair", full[level - len(bits)]))
        for at, (base, bits, full) in enumerate(chunks):
            new, sent, sums = call(
                part(recur_body, opening, at == 0),
                "recur",
                (struct((count, shard), F32), struct((count, shard), BF), struct((24, 128), F32)),
                (*work[at], current[at], previous[at], z[at], sums),
            )
            following.append(new)
            work[at] = (sent, swap(sent, "pair", bits[-1]))
        for level in range(len(chunks[0][1]) - 2, -1, -1):
            for at, (base, bits, full) in enumerate(chunks):
                own, far = work[at]
                packed = call(
                    part(pack_body, bits[level + 1]),
                    "pack",
                    struct((count, 2 * own.shape[1]), BF),
                    (own, far),
                )
                work[at] = (packed, swap(packed, "pair", bits[level]))
        return following, work, sums

    args = scaled_rows(*opening)
    following, gathered, sums = next_vectors(True, args, current, previous, sums)
    previous, current = current, following

    for _ in range(1, ITERS - 1):
        args = scaled_rows(*later_rows(gathered))
        following, gathered, sums = next_vectors(False, args, current, previous, sums)
        previous, current = current, following

    args = scaled_rows(*later_rows(gathered))
    state = [x for pair in zip(current, previous) for x in pair]
    image = call(
        part(image_last_body, chunks, copies, quarter),
        "image_last",
        struct((pair_size, count // pair_size, width), BF),
        (left, right, *args, *state),
        flops // 2,
        [pltpu.VMEM((count, width), F32)],
    )
    got = lax.all_to_all(image, "pair", split_axis=0, concat_axis=0)
    hops = [("aux", 1 << k) for k in range(aux_size.bit_length() - 1)]
    for axis, bit in hops + [("pair", bit) for bit in lower]:
        sums = sums + swap(sums, axis, bit)
    last = call(last_body, "last", struct((count // pair_size, width), F32), (got,))

    divisor = count * width * aux_size
    moments, energy = call(
        functools.partial(finish_body, divisor, cheb_coefficients(ITERS + 1)),
        "finish",
        (struct((1, ITERS + 1), F32), struct((1, 1), F32)),
        (sums, image),
    )
    moments, energy = moments.reshape(ITERS + 1), energy.reshape(1)
    return (last.T, moments, energy)


def solution(mesh):
    placed = (P("pair", "aux"), P("pair"), P("aux", None))
    return jax.shard_map(
        per_device,
        mesh=mesh,
        in_specs=placed,
        out_specs=(P("aux", "pair"), P(), P()),
        check_vma=False,
    )
```

```python
import functools

import jax
import jax.numpy as jnp
import numpy as np
from jax import lax
from jax.experimental import pallas as pl
from jax.experimental.pallas import tpu as pltpu
from jax.sharding import PartitionSpec as P

ITERS = 8
SUMMED = ITERS // 2


spread = 5.0


BF = jnp.bfloat16
F32 = jnp.float32
VM = pl.BlockSpec(memory_space=pltpu.VMEM)
TILE = 512
PIECE = 256


def cheb_coefficients(order_count):
    node_count = 64
    angles = (np.arange(node_count) + 0.5) * np.pi / node_count
    samples = np.log(1.0 + spread * (np.cos(angles) + 1.0) / 2.0)
    values = [
        2.0 / node_count * np.sum(samples * np.cos(degree * angles))
        for degree in range(order_count)
    ]
    values[0] = values[0] / 2.0
    return np.array(values)


def call(body, name, outs, args, flops=0, scratch=(), limit=8, specs=None):
    moved = sum(a.size * a.dtype.itemsize for a in args)
    return pl.pallas_call(
        body,
        out_shape=outs,
        in_specs=specs or [VM] * len(args),
        out_specs=jax.tree.map(lambda _: VM, outs),
        scratch_shapes=scratch,
        compiler_params=pltpu.CompilerParams(vmem_limit_bytes=limit << 20),
        cost_estimate=pl.CostEstimate(flops=flops, bytes_accessed=moved, transcendentals=0),
        name=name,
    )(*args)


def struct(shape, dtype):
    return jax.ShapeDtypeStruct(shape, dtype)


def swap(x, axis, bit):
    size = lax.axis_size(axis)
    return lax.ppermute(x, axis, [(i, i ^ bit) for i in range(size)])


def bit_of(axis, bit):
    return lax.rem(lax.div(lax.axis_index(axis), jnp.int32(bit)), jnp.int32(2))


def span(start, size):
    return pl.ds(pl.multiple_of(start, size), size)


def tiles(width, tile, step, unroll=1):
    def run(k, carry):
        step(pl.multiple_of(k * tile, tile))
        return carry

    lax.fori_loop(0, width // tile, run, 0, unroll=min(unroll, width // tile))


def start_body(chunks, b, wide, w, left, right, turned_left, turned_right, give, keep, weights, sums, *refs):
    shards, (v, sems) = refs[:-2], refs[-2:]
    sums[...] = jnp.zeros_like(sums)
    pairs, width = b.shape
    half = pairs // 2
    core = bit_of("aux", 1)

    sides = ((left, turned_left, 0), (right, turned_right, left.shape[1]))

    def copy(k, side):
        held, _, base = side
        at = span(lax.rem((1 - core) * half + k * PIECE, pairs), PIECE)
        source = b.at[at, base : base + held.shape[1]]
        return pltpu.make_async_copy(source, held.at[at], sems.at[k, 0 if base == 0 else 1]), at

    for k in range(pairs // PIECE):
        for side in sides:
            copy(k, side)[0].start()
    v[...] = wide[...].astype(BF)
    weights[...] = w[:, span(core * half, half)]
    for (base, bits, _), z in zip(chunks, shards):
        z[...] = wide[:, span(shard_start(base, bits, width // len(chunks)), z.shape[1])]

    for part, out in enumerate((give, keep)):
        first = part * out.shape[1] // PIECE

        def step(n, out=out, first=first):
            k = lax.div(n, jnp.int32(PIECE))
            acc = 0.0
            for side in sides:
                move, at = copy(k + first, side)
                move.wait()
                held, turned, base = side
                for c in range(0, turned.shape[0], PIECE):
                    turned[c : c + PIECE, at] = held[at, c : c + PIECE].T
                cols = v[:, base : base + turned.shape[0]]
                acc = acc + jnp.dot(cols, turned[:, at], preferred_element_type=F32)
            out[:, pl.ds(n, PIECE)] = acc.astype(out.dtype)

        tiles(out.shape[1], PIECE, step)


def side_of(bit, width, far):
    mine = bit_of("pair", bit)
    return span(((1 - mine) if far else mine) * width, width)


def rows_own_body(bits, left, right, own_left, own_right, o):
    tile = min(TILE, o.shape[1])
    near = [side_of(bit, own.shape[1], False) for bit, own in zip(bits, (own_left, own_right))]

    def step(n):
        at = pl.ds(n, tile)
        acc = jnp.dot(own_left[...], left[near[0], at], preferred_element_type=F32)
        o[:, at] = acc + jnp.dot(own_right[...], right[near[1], at], preferred_element_type=F32)

    tiles(o.shape[1], tile, step)


def rows_far_body(bit, turned, far, before, o):
    tile = min(TILE, o.shape[1])
    side = side_of(bit, far.shape[1], True)

    def step(n):
        at = pl.ds(n, tile)
        o[:, at] = before[:, at] + jnp.dot(far[...], turned[side, at], preferred_element_type=F32)

    tiles(o.shape[1], tile, step)


def rows_end_body(bit, keep, turned, far, before, o):
    tile = min(TILE, o.shape[1])
    core = bit_of("aux", 1)
    start = (core if keep else 1 - core) * o.shape[1]
    side = side_of(bit, far.shape[1], True)

    def step(n):
        at = span(start + n, tile)
        acc = before[:, at] + jnp.dot(far[...], turned[side, at], preferred_element_type=F32)
        o[:, pl.ds(n, tile)] = acc.astype(o.dtype)

    tiles(o.shape[1], tile, step, 2)


def add_body(keep, got, total, sent):
    t = keep[...] + got[...].astype(F32)
    total[...] = t
    sent[...] = t.astype(BF)


def scale_body(total, got, w, *refs):
    refs[-1][...] = (w[...] * (total[...] + got[...].astype(F32))).astype(BF)


def image_first_body(left, right, own, o):
    width, half = left.shape[1], own.shape[1]
    at = span(bit_of("aux", 1) * half, half)

    def step(n):
        for b, base in ((left, 0), (right, width)):
            acc = jnp.dot(own[...], b[at, pl.ds(n, TILE)], preferred_element_type=F32)
            o[:, pl.ds(pl.multiple_of(base + n, TILE), TILE)] = acc

    tiles(width, TILE, step, 2)


def image_dot(b, far, cols):
    half = far.shape[1]
    at = span((1 - bit_of("aux", 1)) * half, half)
    return jnp.dot(far[...], b[at, cols], preferred_element_type=F32)


def image_second_body(region, keep, b, far, first, o):
    base, bit = region
    width = o.shape[1]
    tile = min(TILE, width)
    mine = bit_of("pair", bit)
    part = mine if keep else 1 - mine

    def step(n):
        acc = image_dot(b, far, span(part * width + n, tile))
        acc = first[:, span(base + part * width + n, tile)] + acc
        o[:, pl.ds(n, tile)] = acc.astype(o.dtype)

    tiles(width, tile, step, 1 if keep else 2)


def split_body(bit, keep, got, sent, kept):
    width = kept.shape[1]
    mine = bit_of("pair", bit)
    stay, leave = span(mine * width, width), span((1 - mine) * width, width)
    sent[...] = (keep[:, leave] + got[:, leave].astype(F32)).astype(BF)
    kept[...] = keep[:, stay] + got[:, stay].astype(F32)


def sum_body(keep, got, sent):
    sent[...] = (keep[...].astype(F32) + got[...].astype(F32)).astype(BF)


def pack_body(bit, own, far, o):
    width = own.shape[1]
    mine = bit_of("pair", bit)
    o[:, span(mine * width, width)] = own[...]
    o[:, span((1 - mine) * width, width)] = far[...]


def shard_start(base, bits, width):
    start = base
    for bit in bits:
        width //= 2
        start = start + bit_of("pair", bit) * width
    return start


def picked(k, bit, value):
    return k // bit * 2 * bit + k % bit + value * bit


def image_last_body(base, bits, bit, copies, b, far, first, cur, prev, *refs):
    outs, whole = refs[:-1], refs[-1]
    width = b.shape[1]
    blocks, count, _ = outs[0].shape

    def step(n):
        cols = pl.ds(pl.multiple_of(base + n, TILE), TILE)
        acc = first[:, cols] + image_dot(b, far, pl.ds(n, TILE))
        whole[:, pl.ds(n, TILE)] = (4.0 / spread) * acc

    tiles(width, TILE, step, 2)
    cols = span(shard_start(0, bits, width), cur.shape[1])
    whole[:, cols] = whole[:, cols] - (2.0 / copies) * cur[...] - (1.0 / copies) * prev[...]
    if len(outs) == 1:
        for k in range(blocks):
            outs[0][k] = whole[k * count : (k + 1) * count, :].astype(BF)
        return
    sent, kept = outs
    mine = bit_of("pair", bit)
    for k in range(blocks):
        sent[k] = whole[span(picked(k, bit, 1 - mine) * count, count), :].astype(BF)
        kept[k] = whole[span(picked(k, bit, mine) * count, count), :]


def halve_body(bit, at, keep, got, sent, kept):
    mine = bit_of("pair", bit)
    for k in range(kept.shape[0]):
        leave, stay = picked(k, at, 1 - mine), picked(k, at, mine)
        sent[k] = (keep[leave] + got[leave].astype(F32)).astype(BF)
        kept[k] = keep[stay] + got[stay].astype(F32)


def last_whole_body(*refs):
    ins, o = refs[:-1], refs[-1]
    width = o.shape[1] // len(ins)
    for k, got in enumerate(ins):
        total = got[0].astype(F32)
        for p in range(1, got.shape[0]):
            total = total + got[p].astype(F32)
        o[:, k * width : (k + 1) * width] = total


def last_body(*refs):
    ins, o = refs[:-1], refs[-1]
    width = o.shape[1] // (len(ins) // 2)
    for k in range(len(ins) // 2):
        cols = slice(k * width, (k + 1) * width)
        o[:, cols] = ins[2 * k][0] + ins[2 * k + 1][0].astype(F32)


def lane_sums(x):
    rows = jnp.sum(x, axis=0, keepdims=True)
    out = rows[:, :128]
    for n in range(128, rows.shape[1], 128):
        out = out + rows[:, n : n + 128]
    return out


def recur_body(opening, push, mine, got, cur, prev, *refs):
    image = mine[...].astype(F32) + got[...].astype(F32)
    mapped = (2.0 / spread) * image - cur[...]
    value = mapped if opening else 2.0 * mapped - prev[...]
    if push is None:
        new, sent = refs
    else:
        z, sums_in, new, sent, sums = refs
    new[...] = value
    sent[...] = value.astype(BF)
    if push is None:
        return
    before = z[...] if opening else value
    rows = [z[...] * value, before * cur[...], value * value]
    if push:
        sums[3:] = sums_in[:-3]
    else:
        sums[...] = sums_in[...]
    for k, row in enumerate(rows):
        total = lane_sums(row)
        sums[k : k + 1] = total if push else sums_in[k : k + 1] + total


def tie_body(x, after, o):
    o[...] = x[...]


def finish_body(divisor, coefficients, sums, after, moments, energy):
    totals = jnp.sum(sums[...], axis=1, keepdims=True) / divisor

    def total(order, k):
        row = 3 * (SUMMED - order) + k
        return totals[row : row + 1]

    found = [total(1, 1)] + [total(order, 0) for order in range(1, SUMMED + 1)]
    found += [2.0 * total(order // 2 + order % 2, 2 - order % 2) - found[order % 2] for order in range(SUMMED + 1, ITERS + 1)]
    lane = lax.broadcasted_iota(jnp.int32, moments.shape, 1)
    row = jnp.zeros(moments.shape, F32)
    weighed = jnp.zeros(energy.shape, F32)
    for k, coefficient in enumerate(coefficients):
        row = jnp.where(lane == k, found[k], row)
        weighed = weighed + float(coefficient) * found[k]
    moments[...] = row
    energy[...] = weighed


def per_device(pair_factors, pair_weights, probes):
    aux_size, pair_size = lax.axis_size("aux"), lax.axis_size("pair")
    pairs, width = pair_factors.shape
    count = probes.shape[1]
    half = pairs // 2
    flops = 2 * pairs * width * count
    part = functools.partial

    order = [1 << k for k in range(pair_size.bit_length() - 1)]
    top, lower = order[-1], order[:-1]
    chunk_width = width // 2
    chunks = [
        (0, lower[::-1], [top]),
        (chunk_width, lower, [top]),
    ]
    copies = 2
    shard = chunk_width * copies // pair_size

    left, right, turned_left, turned_right, *opening, weights, sums, z_left, z_right = call(
        part(start_body, chunks),
        "start",
        (
            pltpu.VMEM((pairs, chunk_width), BF),
            pltpu.VMEM((pairs, chunk_width), BF),
            pltpu.VMEM((chunk_width, pairs), BF),
            pltpu.VMEM((chunk_width, pairs), BF),
            struct((count, half), BF),
            struct((count, half), F32),
            struct((1, half), F32),
            struct((16, 128), F32),
            *[struct((count, shard), F32) for _ in chunks],
        ),
        (pair_factors, probes.T, pair_weights[None, :]),
        flops,
        [pltpu.VMEM((count, width), BF), pltpu.SemaphoreType.DMA((pairs // PIECE, 2))],
        20,
        [pl.BlockSpec(memory_space=pltpu.HBM), VM, VM],
    )
    z = [z_left, z_right]
    previous, current = list(z), list(z)
    hops = [("aux", 1 << k) for k in range(aux_size.bit_length() - 1)]
    hops += [("pair", bit) for bit in lower]
    late = ITERS - SUMMED
    rounds = [hops[k - SUMMED :: late] if k >= SUMMED else [] for k in range(ITERS)]
    outs = (struct((count, half), F32), struct((count, half), BF))

    def later_rows(gathered):
        (own_left, far_left), (own_right, far_right) = gathered
        bits = [chunk[1][0] for chunk in chunks]
        whole = struct((count, pairs), F32)
        rows = call(
            part(rows_own_body, bits),
            "rows_own",
            whole,
            (turned_left, turned_right, own_left, own_right),
            flops // 2,
        )
        rows = call(
            part(rows_far_body, bits[0]), "rows_far", whole, (turned_left, far_left, rows), flops // 4
        )
        args = (turned_right, far_right, rows)
        return [
            call(
                part(rows_end_body, bits[1], keep),
                "rows_keep" if keep else "rows_give",
                struct((count, half), F32 if keep else BF),
                args,
                flops // 8,
            )
            for keep in (False, True)
        ]

    def scaled_rows(degree, sums, give, total):
        got = swap(give, "aux", 1)
        bit = 2
        while bit < aux_size:
            total, sent = call(add_body, "add", outs, (total, got))
            got = swap(sent, "aux", bit)
            bit *= 2
        for axis, bit in rounds[degree]:
            tied = call(tie_body, "tie", struct(sums.shape, F32), (sums, sent))
            sums = tied + swap(tied, axis, bit)
        order = [sums] * bool(rounds[degree])
        own = call(scale_body, "scale", struct((count, half), BF), (total, got, weights, *order))
        far = swap(own, "aux", 1)
        whole = struct((count, width), F32)
        image = call(image_first_body, "image_first", whole, (left, right, own), flops // 2)
        return sums, (far, image)

    piece = chunk_width // 2

    def next_vectors(degree, args, current, previous, sums):
        work, following = [], []
        sides = ((left, *args), (right, *args))
        for side, (base, bits, full) in zip(sides, chunks):
            body = part(image_second_body, (base, bits[0]))
            sent = call(
                part(body, False), "image_give", struct((count, piece), BF), side, flops // 8
            )
            got = swap(sent, "pair", bits[0])
            work.append((sent, got))
        for at, (base, bits, full) in enumerate(chunks):
            body = part(image_second_body, (base, bits[0]))
            kept = call(
                part(body, True),
                "image_keep",
                struct((count, piece), F32),
                sides[at],
                flops // 8,
            )
            work[at] = (kept, work[at][1])
        for level in range(1, pair_size.bit_length() - 1):
            for at, (base, bits, full) in enumerate(chunks):
                if level < len(bits):
                    size = chunk_width >> (level + 1)
                    sent, kept = call(
                        part(split_body, bits[level]),
                        "split",
                        (struct((count, size), BF), struct((count, size), F32)),
                        work[at],
                    )
                    work[at] = (kept, swap(sent, "pair", bits[level]))
                else:
                    sent = call(sum_body, "sum", struct((count, shard), BF), work[at])
                    work[at] = (sent, swap(sent, "pair", full[level - len(bits)]))
        summed = degree < SUMMED
        for at, (base, bits, full) in enumerate(chunks):
            made = call(
                part(recur_body, degree == 0, at == 0 if summed else None),
                "recur",
                (
                    struct((count, shard), F32),
                    struct((count, shard), BF),
                    *[struct(sums.shape, F32)] * summed,
                ),
                (*work[at], current[at], previous[at], *((z[at], sums) if summed else ())),
            )
            new, sent = made[:2]
            sums = made[2] if summed else sums
            following.append(new)
            work[at] = (sent, swap(sent, "pair", bits[-1]))
        for level in range(len(chunks[0][1]) - 2, -1, -1):
            for at, (base, bits, full) in enumerate(chunks):
                own, far = work[at]
                packed = call(
                    part(pack_body, bits[level + 1]),
                    "pack",
                    struct((count, 2 * own.shape[1]), BF),
                    (own, far),
                )
                work[at] = (packed, swap(packed, "pair", bits[level]))
        return following, work, sums

    for degree in range(ITERS):
        rows = later_rows(gathered) if degree else opening
        sums, args = scaled_rows(degree, sums, *rows)
        if degree < ITERS - 1:
            following, gathered, sums = next_vectors(degree, args, current, previous, sums)
            previous, current = current, following

    blocks, each = pair_size // 2, count // pair_size
    work, left_bits = [], []
    by_halves = each % 8 == 0
    for at, (side, (base, bits, full)) in enumerate(zip((left, right), chunks)):
        if by_halves:
            outs = [struct((blocks, each, chunk_width), kind) for kind in (BF, F32)]
        else:
            outs = [struct((pair_size, each, chunk_width), BF)]
        sent, *kept = call(
            part(image_last_body, base, bits, bits[0], copies),
            "image_last",
            outs,
            (side, *args, current[at], previous[at]),
            flops // 4,
            [pltpu.VMEM((count, chunk_width), F32)],
        )
        if not by_halves:
            work.append([lax.all_to_all(sent, "pair", split_axis=0, concat_axis=0)])
            continue
        work.append((kept[0], swap(sent, "pair", bits[0])))
        left_bits.append(sorted(set(bits + full) - {bits[0]}))
    while by_halves and blocks > 1:
        blocks //= 2
        for at, (base, bits, full) in enumerate(chunks):
            bit = [x for x in bits + full if x in left_bits[at]][0]
            sent, kept = call(
                part(halve_body, bit, 1 << left_bits[at].index(bit)),
                "halve",
                (struct((blocks, each, chunk_width), BF), struct((blocks, each, chunk_width), F32)),
                work[at],
            )
            left_bits[at].remove(bit)
            work[at] = (kept, swap(sent, "pair", bit))
    args = [x for pair in work for x in pair]
    last = call(last_body if by_halves else last_whole_body, "last", struct((each, width), F32), args)

    divisor = count * width * aux_size
    moments, energy = call(
        functools.partial(finish_body, divisor, cheb_coefficients(ITERS + 1)),
        "finish",
        (struct((1, ITERS + 1), F32), struct((1, 1), F32)),
        (sums, work[0][0]),
    )
    moments, energy = moments.reshape(ITERS + 1), energy.reshape(1)
    return (last.T, moments, energy)


def solution(mesh):
    placed = (P("pair", "aux"), P("pair"), P("aux", None))
    return jax.shard_map(
        per_device,
        mesh=mesh,
        in_specs=placed,
        out_specs=(P("aux", "pair"), P(), P()),
        check_vma=False,
    )
```

```python
import functools

import jax
import jax.numpy as jnp
import numpy as np
from jax import lax
from jax.experimental import pallas as pl
from jax.experimental.pallas import tpu as pltpu
from jax.sharding import PartitionSpec as P

ITERS = 8
SUMMED = ITERS // 2


spread = 5.0


BF = jnp.bfloat16
F32 = jnp.float32
VM = pl.BlockSpec(memory_space=pltpu.VMEM)
TILE = 512
PIECE = 256


def cheb_coefficients(order_count):
    node_count = 64
    angles = (np.arange(node_count) + 0.5) * np.pi / node_count
    samples = np.log(1.0 + spread * (np.cos(angles) + 1.0) / 2.0)
    values = [
        2.0 / node_count * np.sum(samples * np.cos(degree * angles))
        for degree in range(order_count)
    ]
    values[0] = values[0] / 2.0
    return np.array(values)


def call(body, name, outs, args, flops=0, scratch=(), limit=8, specs=None):
    moved = sum(a.size * a.dtype.itemsize for a in args)
    return pl.pallas_call(
        body,
        out_shape=outs,
        in_specs=specs or [VM] * len(args),
        out_specs=jax.tree.map(lambda _: VM, outs),
        scratch_shapes=scratch,
        compiler_params=pltpu.CompilerParams(vmem_limit_bytes=limit << 20),
        cost_estimate=pl.CostEstimate(flops=flops, bytes_accessed=moved, transcendentals=0),
        name=name,
    )(*args)


def struct(shape, dtype):
    return jax.ShapeDtypeStruct(shape, dtype)


def swap(x, axis, bit):
    size = lax.axis_size(axis)
    return lax.ppermute(x, axis, [(i, i ^ bit) for i in range(size)])


def bit_of(axis, bit):
    return lax.rem(lax.div(lax.axis_index(axis), jnp.int32(bit)), jnp.int32(2))


def span(start, size):
    return pl.ds(pl.multiple_of(start, size), size)


def tiles(width, tile, step, unroll=1):
    def run(k, carry):
        step(pl.multiple_of(k * tile, tile))
        return carry

    lax.fori_loop(0, width // tile, run, 0, unroll=min(unroll, width // tile))


def start_body(chunks, b, wide, w, left, right, turned_left, turned_right, give, keep, weights, sums, *refs):
    shards, (v, sems) = refs[:-2], refs[-2:]
    sums[...] = jnp.zeros_like(sums)
    pairs, width = b.shape
    half = pairs // 2
    core = bit_of("aux", 1)

    sides = ((left, turned_left, 0), (right, turned_right, left.shape[1]))

    def copy(k, side):
        held, _, base = side
        at = span(lax.rem((1 - core) * half + k * PIECE, pairs), PIECE)
        source = b.at[at, base : base + held.shape[1]]
        return pltpu.make_async_copy(source, held.at[at], sems.at[k, 0 if base == 0 else 1]), at

    for k in range(pairs // PIECE):
        for side in sides:
            copy(k, side)[0].start()
    v[...] = wide[...].astype(BF)
    weights[...] = w[:, span(core * half, half)]
    for (base, bits, _), z in zip(chunks, shards):
        z[...] = wide[:, span(shard_start(base, bits, width // len(chunks)), z.shape[1])]

    for part, out in enumerate((give, keep)):
        first = part * out.shape[1] // PIECE

        def step(n, out=out, first=first):
            k = lax.div(n, jnp.int32(PIECE))
            acc = 0.0
            for side in sides:
                move, at = copy(k + first, side)
                move.wait()
                held, turned, base = side
                for c in range(0, turned.shape[0], PIECE):
                    turned[c : c + PIECE, at] = held[at, c : c + PIECE].T
                cols = v[:, base : base + turned.shape[0]]
                acc = acc + jnp.dot(cols, turned[:, at], preferred_element_type=F32)
            out[:, pl.ds(n, PIECE)] = acc.astype(out.dtype)

        tiles(out.shape[1], PIECE, step)


def block_of(step, order):
    block = 0
    for bit in order:
        mine = bit_of("pair", bit)
        block = 2 * block + (1 - mine if step & bit else mine)
    return block


def block_span(step, order, size):
    return span(block_of(step, order) * size, size)


def steps_of(order):
    return list(range((1 << len(order)) - 1, 0, -1))


def rows_own_body(orders, left, right, own_left, own_right, o):
    tile = min(TILE, o.shape[1])
    near = [block_span(0, order, own_left.shape[1]) for order in orders]

    def step(n):
        at = pl.ds(n, tile)
        acc = jnp.dot(own_left[...], left[near[0], at], preferred_element_type=F32)
        o[:, at] = acc + jnp.dot(own_right[...], right[near[1], at], preferred_element_type=F32)

    tiles(o.shape[1], tile, step)


def add_far(order, turned, far, at, acc):
    for step, block in zip(steps_of(order), far):
        side = block_span(step, order, block.shape[1])
        acc = acc + jnp.dot(block[...], turned[side, at], preferred_element_type=F32)
    return acc


def rows_far_body(order, turned, before, *refs):
    far, o = refs[:-1], refs[-1]
    tile = min(TILE, o.shape[1])

    def step(n):
        at = pl.ds(n, tile)
        o[:, at] = add_far(order, turned, far, at, before[:, at])

    tiles(o.shape[1], tile, step)


def rows_end_body(order, keep, turned, before, *refs):
    far, o = refs[:-1], refs[-1]
    tile = min(TILE, o.shape[1])
    core = bit_of("aux", 1)
    start = (core if keep else 1 - core) * o.shape[1]

    def step(n):
        at = span(start + n, tile)
        o[:, pl.ds(n, tile)] = add_far(order, turned, far, at, before[:, at]).astype(o.dtype)

    tiles(o.shape[1], tile, step, 2)


def add_body(keep, got, total, sent):
    t = keep[...] + got[...].astype(F32)
    total[...] = t
    sent[...] = t.astype(BF)


def scale_body(total, got, w, *refs):
    refs[-1][...] = (w[...] * (total[...] + got[...].astype(F32))).astype(BF)


def image_first_body(left, right, own, o):
    width, half = left.shape[1], own.shape[1]
    at = span(bit_of("aux", 1) * half, half)

    def step(n):
        for b, base in ((left, 0), (right, width)):
            acc = jnp.dot(own[...], b[at, pl.ds(n, TILE)], preferred_element_type=F32)
            o[:, pl.ds(pl.multiple_of(base + n, TILE), TILE)] = acc

    tiles(width, TILE, step, 2)


def image_dot(b, far, cols):
    half = far.shape[1]
    at = span((1 - bit_of("aux", 1)) * half, half)
    return jnp.dot(far[...], b[at, cols], preferred_element_type=F32)


def image_second_body(region, keep, b, far, first, o):
    base, bit = region
    width = o.shape[1]
    tile = min(TILE, width)
    mine = bit_of("pair", bit)
    part = mine if keep else 1 - mine

    def step(n):
        acc = image_dot(b, far, span(part * width + n, tile))
        acc = first[:, span(base + part * width + n, tile)] + acc
        o[:, pl.ds(n, tile)] = acc.astype(o.dtype)

    tiles(width, tile, step, 1 if keep else 2)


def split_body(bit, keep, got, sent, kept):
    width = kept.shape[1]
    mine = bit_of("pair", bit)
    stay, leave = span(mine * width, width), span((1 - mine) * width, width)
    sent[...] = (keep[:, leave] + got[:, leave].astype(F32)).astype(BF)
    kept[...] = keep[:, stay] + got[:, stay].astype(F32)


def sum_body(keep, got, sent):
    sent[...] = (keep[...].astype(F32) + got[...].astype(F32)).astype(BF)


def shard_start(base, bits, width):
    start = base
    for bit in bits:
        width //= 2
        start = start + bit_of("pair", bit) * width
    return start


def picked(k, bit, value):
    return k // bit * 2 * bit + k % bit + value * bit


def image_last_body(base, bits, bit, copies, b, far, first, cur, prev, *refs):
    outs, whole = refs[:-1], refs[-1]
    width = b.shape[1]
    blocks, count, _ = outs[0].shape

    def step(n):
        cols = pl.ds(pl.multiple_of(base + n, TILE), TILE)
        acc = first[:, cols] + image_dot(b, far, pl.ds(n, TILE))
        whole[:, pl.ds(n, TILE)] = (4.0 / spread) * acc

    tiles(width, TILE, step, 2)
    cols = span(shard_start(0, bits, width), cur.shape[1])
    whole[:, cols] = whole[:, cols] - (2.0 / copies) * cur[...] - (1.0 / copies) * prev[...]
    if len(outs) == 1:
        for k in range(blocks):
            outs[0][k] = whole[k * count : (k + 1) * count, :].astype(BF)
        return
    sent, kept = outs
    mine = bit_of("pair", bit)
    for k in range(blocks):
        sent[k] = whole[span(picked(k, bit, 1 - mine) * count, count), :].astype(BF)
        kept[k] = whole[span(picked(k, bit, mine) * count, count), :]


def halve_body(bit, at, keep, got, sent, kept):
    mine = bit_of("pair", bit)
    for k in range(kept.shape[0]):
        leave, stay = picked(k, at, 1 - mine), picked(k, at, mine)
        sent[k] = (keep[leave] + got[leave].astype(F32)).astype(BF)
        kept[k] = keep[stay] + got[stay].astype(F32)


def last_whole_body(*refs):
    ins, o = refs[:-1], refs[-1]
    width = o.shape[1] // len(ins)
    for k, got in enumerate(ins):
        total = got[0].astype(F32)
        for p in range(1, got.shape[0]):
            total = total + got[p].astype(F32)
        o[:, k * width : (k + 1) * width] = total


def last_body(*refs):
    ins, o = refs[:-1], refs[-1]
    width = o.shape[1] // (len(ins) // 2)
    for k in range(len(ins) // 2):
        cols = slice(k * width, (k + 1) * width)
        o[:, cols] = ins[2 * k][0] + ins[2 * k + 1][0].astype(F32)


def lane_sums(x):
    rows = jnp.sum(x, axis=0, keepdims=True)
    out = rows[:, :128]
    for n in range(128, rows.shape[1], 128):
        out = out + rows[:, n : n + 128]
    return out


def recur_body(opening, push, mine, got, cur, prev, *refs):
    image = mine[...].astype(F32) + got[...].astype(F32)
    mapped = (2.0 / spread) * image - cur[...]
    value = mapped if opening else 2.0 * mapped - prev[...]
    if push is None:
        new, sent = refs
    else:
        z, sums_in, new, sent, sums = refs
    new[...] = value
    sent[...] = value.astype(BF)
    if push is None:
        return
    before = z[...] if opening else value
    rows = [z[...] * value, before * cur[...], value * value]
    if push:
        sums[3:] = sums_in[:-3]
    else:
        sums[...] = sums_in[...]
    for k, row in enumerate(rows):
        total = lane_sums(row)
        sums[k : k + 1] = total if push else sums_in[k : k + 1] + total


def tie_body(x, after, o):
    o[...] = x[...]


def finish_body(divisor, coefficients, sums, after, moments, energy):
    totals = jnp.sum(sums[...], axis=1, keepdims=True) / divisor

    def total(order, k):
        row = 3 * (SUMMED - order) + k
        return totals[row : row + 1]

    found = [total(1, 1)] + [total(order, 0) for order in range(1, SUMMED + 1)]
    found += [2.0 * total(order // 2 + order % 2, 2 - order % 2) - found[order % 2] for order in range(SUMMED + 1, ITERS + 1)]
    lane = lax.broadcasted_iota(jnp.int32, moments.shape, 1)
    row = jnp.zeros(moments.shape, F32)
    weighed = jnp.zeros(energy.shape, F32)
    for k, coefficient in enumerate(coefficients):
        row = jnp.where(lane == k, found[k], row)
        weighed = weighed + float(coefficient) * found[k]
    moments[...] = row
    energy[...] = weighed


def per_device(pair_factors, pair_weights, probes):
    aux_size, pair_size = lax.axis_size("aux"), lax.axis_size("pair")
    pairs, width = pair_factors.shape
    count = probes.shape[1]
    half = pairs // 2
    flops = 2 * pairs * width * count
    part = functools.partial

    order = [1 << k for k in range(pair_size.bit_length() - 1)]
    lower, beyond = order[:2], order[2:]
    chunk_width = width // 2
    chunks = [(0, lower[::-1], beyond), (chunk_width, lower, beyond)]
    copies = 1 << len(beyond)
    shard = chunk_width * copies // pair_size

    left, right, turned_left, turned_right, *opening, weights, sums, z_left, z_right = call(
        part(start_body, chunks),
        "start",
        (
            pltpu.VMEM((pairs, chunk_width), BF),
            pltpu.VMEM((pairs, chunk_width), BF),
            pltpu.VMEM((chunk_width, pairs), BF),
            pltpu.VMEM((chunk_width, pairs), BF),
            struct((count, half), BF),
            struct((count, half), F32),
            struct((1, half), F32),
            struct((16, 128), F32),
            *[struct((count, shard), F32) for _ in chunks],
        ),
        (pair_factors, probes.T, pair_weights[None, :]),
        flops,
        [pltpu.VMEM((count, width), BF), pltpu.SemaphoreType.DMA((pairs // PIECE, 2))],
        20,
        [pl.BlockSpec(memory_space=pltpu.HBM), VM, VM],
    )
    z = [z_left, z_right]
    previous, current = list(z), list(z)
    hops = [("aux", 1 << k) for k in range(aux_size.bit_length() - 1)]
    hops += [("pair", bit) for bit in lower]
    late = ITERS - SUMMED
    rounds = [hops[k - SUMMED :: late] if k >= SUMMED else [] for k in range(ITERS)]
    outs = (struct((count, half), F32), struct((count, half), BF))

    def later_rows(gathered):
        (own_left, far_left), (own_right, far_right) = gathered
        whole = struct((count, pairs), F32)
        orders = [bits for _, bits, _ in chunks]
        rows = call(
            part(rows_own_body, orders),
            "rows_own",
            whole,
            (turned_left, turned_right, own_left, own_right),
            flops // 4,
        )
        rows = call(
            part(rows_far_body, orders[0]),
            "rows_far",
            whole,
            (turned_left, rows, *far_left),
            flops // 3,
        )
        args = (turned_right, rows, *far_right)
        return [
            call(
                part(rows_end_body, orders[1], keep),
                "rows_keep" if keep else "rows_give",
                struct((count, half), F32 if keep else BF),
                args,
                flops // 8,
            )
            for keep in (False, True)
        ]

    def scaled_rows(degree, sums, give, total):
        got = swap(give, "aux", 1)
        bit = 2
        while bit < aux_size:
            total, sent = call(add_body, "add", outs, (total, got))
            got = swap(sent, "aux", bit)
            bit *= 2
        for axis, bit in rounds[degree]:
            tied = call(tie_body, "tie", struct(sums.shape, F32), (sums, sent))
            sums = tied + swap(tied, axis, bit)
        order = [sums] * bool(rounds[degree])
        own = call(scale_body, "scale", struct((count, half), BF), (total, got, weights, *order))
        far = swap(own, "aux", 1)
        whole = struct((count, width), F32)
        image = call(image_first_body, "image_first", whole, (left, right, own), flops // 2)
        return sums, (far, image)

    piece = chunk_width // 2

    def next_vectors(degree, args, current, previous, sums):
        work, following = [], []
        sides = ((left, *args), (right, *args))
        for side, (base, bits, full) in zip(sides, chunks):
            body = part(image_second_body, (base, bits[0]))
            sent = call(
                part(body, False), "image_give", struct((count, piece), BF), side, flops // 8
            )
            got = swap(sent, "pair", bits[0])
            work.append((sent, got))
        for at, (base, bits, full) in enumerate(chunks):
            body = part(image_second_body, (base, bits[0]))
            kept = call(
                part(body, True),
                "image_keep",
                struct((count, piece), F32),
                sides[at],
                flops // 8,
            )
            work[at] = (kept, work[at][1])
        for level in range(1, pair_size.bit_length() - 1):
            for at, (base, bits, full) in enumerate(chunks):
                if level < len(bits):
                    size = chunk_width >> (level + 1)
                    sent, kept = call(
                        part(split_body, bits[level]),
                        "split",
                        (struct((count, size), BF), struct((count, size), F32)),
                        work[at],
                    )
                    work[at] = (kept, swap(sent, "pair", bits[level]))
                else:
                    sent = call(sum_body, "sum", struct((count, shard), BF), work[at])
                    work[at] = (sent, swap(sent, "pair", full[level - len(bits)]))
        summed = degree < SUMMED
        for at, (base, bits, full) in enumerate(chunks):
            made = call(
                part(recur_body, degree == 0, at == 0 if summed else None),
                "recur",
                (
                    struct((count, shard), F32),
                    struct((count, shard), BF),
                    *[struct(sums.shape, F32)] * summed,
                ),
                (*work[at], current[at], previous[at], *((z[at], sums) if summed else ())),
            )
            new, sent = made[:2]
            sums = made[2] if summed else sums
            following.append(new)
            work[at] = (sent, [swap(sent, "pair", step) for step in steps_of(bits)])
        return following, work, sums

    for degree in range(ITERS):
        rows = later_rows(gathered) if degree else opening
        sums, args = scaled_rows(degree, sums, *rows)
        if degree < ITERS - 1:
            following, gathered, sums = next_vectors(degree, args, current, previous, sums)
            previous, current = current, following

    blocks, each = pair_size // 2, count // pair_size
    work, left_bits = [], []
    by_halves = each % 8 == 0
    for at, (side, (base, bits, full)) in enumerate(zip((left, right), chunks)):
        if by_halves:
            outs = [struct((blocks, each, chunk_width), kind) for kind in (BF, F32)]
        else:
            outs = [struct((pair_size, each, chunk_width), BF)]
        sent, *kept = call(
            part(image_last_body, base, bits, bits[0], copies),
            "image_last",
            outs,
            (side, *args, current[at], previous[at]),
            flops // 4,
            [pltpu.VMEM((count, chunk_width), F32)],
        )
        if not by_halves:
            work.append([lax.all_to_all(sent, "pair", split_axis=0, concat_axis=0)])
            continue
        work.append((kept[0], swap(sent, "pair", bits[0])))
        left_bits.append(sorted(set(bits + full) - {bits[0]}))
    while by_halves and blocks > 1:
        blocks //= 2
        for at, (base, bits, full) in enumerate(chunks):
            bit = [x for x in bits + full if x in left_bits[at]][0]
            sent, kept = call(
                part(halve_body, bit, 1 << left_bits[at].index(bit)),
                "halve",
                (struct((blocks, each, chunk_width), BF), struct((blocks, each, chunk_width), F32)),
                work[at],
            )
            left_bits[at].remove(bit)
            work[at] = (kept, swap(sent, "pair", bit))
    args = [x for pair in work for x in pair]
    last = call(last_body if by_halves else last_whole_body, "last", struct((each, width), F32), args)

    divisor = count * width * aux_size
    moments, energy = call(
        functools.partial(finish_body, divisor, cheb_coefficients(ITERS + 1)),
        "finish",
        (struct((1, ITERS + 1), F32), struct((1, 1), F32)),
        (sums, work[0][0]),
    )
    moments, energy = moments.reshape(ITERS + 1), energy.reshape(1)
    return (last.T, moments, energy)


def solution(mesh):
    placed = (P("pair", "aux"), P("pair"), P("aux", None))
    return jax.shard_map(
        per_device,
        mesh=mesh,
        in_specs=placed,
        out_specs=(P("aux", "pair"), P(), P()),
        check_vma=False,
    )
```

```python
import functools

import jax
import jax.numpy as jnp
import numpy as np
from jax import lax
from jax.experimental import pallas as pl
from jax.experimental.pallas import tpu as pltpu
from jax.sharding import PartitionSpec as P

ITERS = 8
SUMMED = ITERS // 2


spread = 5.0


BF = jnp.bfloat16
F32 = jnp.float32
VM = pl.BlockSpec(memory_space=pltpu.VMEM)
TILE = 512
PIECE = 256


def cheb_coefficients(order_count):
    node_count = 64
    angles = (np.arange(node_count) + 0.5) * np.pi / node_count
    samples = np.log(1.0 + spread * (np.cos(angles) + 1.0) / 2.0)
    values = [
        2.0 / node_count * np.sum(samples * np.cos(degree * angles))
        for degree in range(order_count)
    ]
    values[0] = values[0] / 2.0
    return np.array(values)


def call(body, name, outs, args, flops=0, scratch=(), limit=8, specs=None):
    moved = sum(a.size * a.dtype.itemsize for a in args)
    return pl.pallas_call(
        body,
        out_shape=outs,
        in_specs=specs or [VM] * len(args),
        out_specs=jax.tree.map(lambda _: VM, outs),
        scratch_shapes=scratch,
        compiler_params=pltpu.CompilerParams(vmem_limit_bytes=limit << 20),
        cost_estimate=pl.CostEstimate(flops=flops, bytes_accessed=moved, transcendentals=0),
        name=name,
    )(*args)


def struct(shape, dtype):
    return jax.ShapeDtypeStruct(shape, dtype)


def swap(x, axis, bit):
    size = lax.axis_size(axis)
    return lax.ppermute(x, axis, [(i, i ^ bit) for i in range(size)])


def bit_of(axis, bit):
    return lax.rem(lax.div(lax.axis_index(axis), jnp.int32(bit)), jnp.int32(2))


def span(start, size):
    return pl.ds(pl.multiple_of(start, size), size)


def tiles(width, tile, step, unroll=1):
    def run(k, carry):
        step(pl.multiple_of(k * tile, tile))
        return carry

    lax.fori_loop(0, width // tile, run, 0, unroll=min(unroll, width // tile))


def start_body(chunks, b, wide, w, left, right, turned_left, turned_right, give, keep, weights, sums, *refs):
    shards, (v, sems) = refs[:-2], refs[-2:]
    sums[...] = jnp.zeros_like(sums)
    pairs, width = b.shape
    half = pairs // 2
    core = bit_of("aux", 1)

    sides = ((left, turned_left, 0), (right, turned_right, left.shape[1]))

    def copy(k, side):
        held, _, base = side
        at = span(lax.rem((1 - core) * half + k * PIECE, pairs), PIECE)
        source = b.at[at, base : base + held.shape[1]]
        return pltpu.make_async_copy(source, held.at[at], sems.at[k, 0 if base == 0 else 1]), at

    for k in range(pairs // PIECE):
        for side in sides:
            copy(k, side)[0].start()
    v[...] = wide[...].astype(BF)
    weights[...] = w[:, span(core * half, half)]
    for (base, bits, _), z in zip(chunks, shards):
        z[...] = wide[:, span(shard_start(base, bits, width // len(chunks)), z.shape[1])]

    for part, out in enumerate((give, keep)):
        first = part * out.shape[1] // PIECE

        def step(n, out=out, first=first):
            k = lax.div(n, jnp.int32(PIECE))
            acc = 0.0
            for side in sides:
                move, at = copy(k + first, side)
                move.wait()
                held, turned, base = side
                for c in range(0, turned.shape[0], PIECE):
                    turned[c : c + PIECE, at] = held[at, c : c + PIECE].T
                cols = v[:, base : base + turned.shape[0]]
                acc = acc + jnp.dot(cols, turned[:, at], preferred_element_type=F32)
            out[:, pl.ds(n, PIECE)] = acc.astype(out.dtype)

        tiles(out.shape[1], PIECE, step)


def block_of(step, order):
    block = 0
    for bit in order:
        mine = bit_of("pair", bit)
        block = 2 * block + (1 - mine if step & bit else mine)
    return block


def block_span(step, order, size):
    return span(block_of(step, order) * size, size)


def steps_of(order):
    return list(range((1 << len(order)) - 1, 0, -1))


def rows_own_body(orders, left, right, own_left, own_right, o):
    tile = min(TILE, o.shape[1])
    near = [block_span(0, order, own_left.shape[1]) for order in orders]

    def step(n):
        at = pl.ds(n, tile)
        acc = jnp.dot(own_left[...], left[near[0], at], preferred_element_type=F32)
        o[:, at] = acc + jnp.dot(own_right[...], right[near[1], at], preferred_element_type=F32)

    tiles(o.shape[1], tile, step)


def add_far(order, turned, far, at, acc):
    for step, block in zip(steps_of(order), far):
        side = block_span(step, order, block.shape[1])
        acc = acc + jnp.dot(block[...], turned[side, at], preferred_element_type=F32)
    return acc


def rows_far_body(order, turned, before, *refs):
    far, o = refs[:-1], refs[-1]
    tile = min(TILE, o.shape[1])

    def step(n):
        at = pl.ds(n, tile)
        o[:, at] = add_far(order, turned, far, at, before[:, at])

    tiles(o.shape[1], tile, step, 2)


def rows_end_body(order, keep, turned, before, *refs):
    far, o = refs[:-1], refs[-1]
    tile = min(TILE, o.shape[1])
    core = bit_of("aux", 1)
    start = (core if keep else 1 - core) * o.shape[1]

    def step(n):
        at = span(start + n, tile)
        o[:, pl.ds(n, tile)] = add_far(order, turned, far, at, before[:, at]).astype(o.dtype)

    tiles(o.shape[1], tile, step, 2)


def add_body(keep, got, total, sent):
    t = keep[...] + got[...].astype(F32)
    total[...] = t
    sent[...] = t.astype(BF)


def scale_body(total, got, w, *refs):
    refs[-1][...] = (w[...] * (total[...] + got[...].astype(F32))).astype(BF)


def image_first_body(left, right, own, o):
    width, half = left.shape[1], own.shape[1]
    at = span(bit_of("aux", 1) * half, half)

    def step(n):
        for b, base in ((left, 0), (right, width)):
            acc = jnp.dot(own[...], b[at, pl.ds(n, TILE)], preferred_element_type=F32)
            o[:, pl.ds(pl.multiple_of(base + n, TILE), TILE)] = acc

    tiles(width, TILE, step, 2)


def image_dot(b, far, cols):
    half = far.shape[1]
    at = span((1 - bit_of("aux", 1)) * half, half)
    return jnp.dot(far[...], b[at, cols], preferred_element_type=F32)


def image_second_body(region, keep, b, far, first, o):
    base, bit = region
    width = o.shape[1]
    tile = min(TILE, width)
    mine = bit_of("pair", bit)
    part = mine if keep else 1 - mine

    def step(n):
        acc = image_dot(b, far, span(part * width + n, tile))
        acc = first[:, span(base + part * width + n, tile)] + acc
        o[:, pl.ds(n, tile)] = acc.astype(o.dtype)

    tiles(width, tile, step, 1 if keep else 2)


def split_body(bit, keep, got, sent, kept):
    width = kept.shape[1]
    mine = bit_of("pair", bit)
    stay, leave = span(mine * width, width), span((1 - mine) * width, width)
    sent[...] = (keep[:, leave] + got[:, leave].astype(F32)).astype(BF)
    kept[...] = keep[:, stay] + got[:, stay].astype(F32)


def sum_body(keep, got, sent):
    sent[...] = (keep[...].astype(F32) + got[...].astype(F32)).astype(BF)


def shard_start(base, bits, width):
    start = base
    for bit in bits:
        width //= 2
        start = start + bit_of("pair", bit) * width
    return start


def picked(k, bit, value):
    return k // bit * 2 * bit + k % bit + value * bit


def image_last_body(base, bits, bit, copies, b, far, first, cur, prev, *refs):
    outs, whole = refs[:-1], refs[-1]
    width = b.shape[1]
    blocks, count, _ = outs[0].shape

    def step(n):
        cols = pl.ds(pl.multiple_of(base + n, TILE), TILE)
        acc = first[:, cols] + image_dot(b, far, pl.ds(n, TILE))
        whole[:, pl.ds(n, TILE)] = (4.0 / spread) * acc

    tiles(width, TILE, step, 2)
    cols = span(shard_start(0, bits, width), cur.shape[1])
    whole[:, cols] = whole[:, cols] - (2.0 / copies) * cur[...] - (1.0 / copies) * prev[...]
    if len(outs) == 1:
        for k in range(blocks):
            outs[0][k] = whole[k * count : (k + 1) * count, :].astype(BF)
        return
    sent, kept = outs
    mine = bit_of("pair", bit)
    for k in range(blocks):
        sent[k] = whole[span(picked(k, bit, 1 - mine) * count, count), :].astype(BF)
        kept[k] = whole[span(picked(k, bit, mine) * count, count), :]


def halve_body(bit, at, keep, got, sent, kept):
    mine = bit_of("pair", bit)
    for k in range(kept.shape[0]):
        leave, stay = picked(k, at, 1 - mine), picked(k, at, mine)
        sent[k] = (keep[leave] + got[leave].astype(F32)).astype(BF)
        kept[k] = keep[stay] + got[stay].astype(F32)


def last_whole_body(*refs):
    ins, o = refs[:-1], refs[-1]
    width = o.shape[1] // len(ins)
    for k, got in enumerate(ins):
        total = got[0].astype(F32)
        for p in range(1, got.shape[0]):
            total = total + got[p].astype(F32)
        o[:, k * width : (k + 1) * width] = total


def last_body(*refs):
    ins, o = refs[:-1], refs[-1]
    width = o.shape[1] // (len(ins) // 2)
    for k in range(len(ins) // 2):
        cols = slice(k * width, (k + 1) * width)
        o[:, cols] = ins[2 * k][0] + ins[2 * k + 1][0].astype(F32)


def lane_sums(x):
    rows = jnp.sum(x, axis=0, keepdims=True)
    out = rows[:, :128]
    for n in range(128, rows.shape[1], 128):
        out = out + rows[:, n : n + 128]
    return out


def recur_body(opening, push, mine, got, cur, prev, *refs):
    image = mine[...].astype(F32) + got[...].astype(F32)
    mapped = (2.0 / spread) * image - cur[...]
    value = mapped if opening else 2.0 * mapped - prev[...]
    if push is None:
        new, sent = refs
    else:
        z, sums_in, new, sent, sums = refs
    new[...] = value
    sent[...] = value.astype(BF)
    if push is None:
        return
    before = z[...] if opening else value
    rows = [z[...] * value, before * cur[...], value * value]
    if push:
        sums[3:] = sums_in[:-3]
    else:
        sums[...] = sums_in[...]
    for k, row in enumerate(rows):
        total = lane_sums(row)
        sums[k : k + 1] = total if push else sums_in[k : k + 1] + total


def tie_body(x, after, o):
    o[...] = x[...]


def finish_body(divisor, coefficients, sums, after, moments, energy):
    totals = jnp.sum(sums[...], axis=1, keepdims=True) / divisor

    def total(order, k):
        row = 3 * (SUMMED - order) + k
        return totals[row : row + 1]

    found = [total(1, 1)] + [total(order, 0) for order in range(1, SUMMED + 1)]
    found += [2.0 * total(order // 2 + order % 2, 2 - order % 2) - found[order % 2] for order in range(SUMMED + 1, ITERS + 1)]
    lane = lax.broadcasted_iota(jnp.int32, moments.shape, 1)
    row = jnp.zeros(moments.shape, F32)
    weighed = jnp.zeros(energy.shape, F32)
    for k, coefficient in enumerate(coefficients):
        row = jnp.where(lane == k, found[k], row)
        weighed = weighed + float(coefficient) * found[k]
    moments[...] = row
    energy[...] = weighed


def per_device(pair_factors, pair_weights, probes):
    aux_size, pair_size = lax.axis_size("aux"), lax.axis_size("pair")
    pairs, width = pair_factors.shape
    count = probes.shape[1]
    half = pairs // 2
    flops = 2 * pairs * width * count
    part = functools.partial

    order = [1 << k for k in range(pair_size.bit_length() - 1)]
    lower, beyond = order[:2], order[2:]
    chunk_width = width // 2
    chunks = [(0, lower[::-1], beyond), (chunk_width, lower, beyond)]
    copies = 1 << len(beyond)
    shard = chunk_width * copies // pair_size

    left, right, turned_left, turned_right, *opening, weights, sums, z_left, z_right = call(
        part(start_body, chunks),
        "start",
        (
            pltpu.VMEM((pairs, chunk_width), BF),
            pltpu.VMEM((pairs, chunk_width), BF),
            pltpu.VMEM((chunk_width, pairs), BF),
            pltpu.VMEM((chunk_width, pairs), BF),
            struct((count, half), BF),
            struct((count, half), F32),
            struct((1, half), F32),
            struct((16, 128), F32),
            *[struct((count, shard), F32) for _ in chunks],
        ),
        (pair_factors, probes.T, pair_weights[None, :]),
        flops,
        [pltpu.VMEM((count, width), BF), pltpu.SemaphoreType.DMA((pairs // PIECE, 2))],
        20,
        [pl.BlockSpec(memory_space=pltpu.HBM), VM, VM],
    )
    z = [z_left, z_right]
    previous, current = list(z), list(z)
    hops = [("aux", 1 << k) for k in range(aux_size.bit_length() - 1)]
    hops += [("pair", bit) for bit in lower]
    late = ITERS - SUMMED
    rounds = [hops[k - SUMMED :: late] if k >= SUMMED else [] for k in range(ITERS)]
    outs = (struct((count, half), F32), struct((count, half), BF))

    def later_rows(gathered):
        (own_left, far_left), (own_right, far_right) = gathered
        whole = struct((count, pairs), F32)
        orders = [bits for _, bits, _ in chunks]
        rows = call(
            part(rows_own_body, orders),
            "rows_own",
            whole,
            (turned_left, turned_right, own_left, own_right),
            flops // 4,
        )
        rows = call(
            part(rows_far_body, orders[0]),
            "rows_far",
            whole,
            (turned_left, rows, *far_left),
            flops // 3,
        )
        args = (turned_right, rows, *far_right)
        return [
            call(
                part(rows_end_body, orders[1], keep),
                "rows_keep" if keep else "rows_give",
                struct((count, half), F32 if keep else BF),
                args,
                flops // 8,
            )
            for keep in (False, True)
        ]

    def scaled_rows(degree, sums, give, total):
        got = swap(give, "aux", 1)
        bit = 2
        while bit < aux_size:
            total, sent = call(add_body, "add", outs, (total, got))
            got = swap(sent, "aux", bit)
            bit *= 2
        for axis, bit in rounds[degree]:
            tied = call(tie_body, "tie", struct(sums.shape, F32), (sums, sent))
            sums = tied + swap(tied, axis, bit)
        order = [sums] * bool(rounds[degree])
        own = call(scale_body, "scale", struct((count, half), BF), (total, got, weights, *order))
        far = swap(own, "aux", 1)
        whole = struct((count, width), F32)
        image = call(image_first_body, "image_first", whole, (left, right, own), flops // 2)
        return sums, (far, image)

    piece = chunk_width // 2

    def next_vectors(degree, args, current, previous, sums):
        work, following = [], []
        sides = ((left, *args), (right, *args))
        for side, (base, bits, full) in zip(sides, chunks):
            body = part(image_second_body, (base, bits[0]))
            sent = call(
                part(body, False), "image_give", struct((count, piece), BF), side, flops // 8
            )
            got = swap(sent, "pair", bits[0])
            work.append((sent, got))
        for at, (base, bits, full) in enumerate(chunks):
            body = part(image_second_body, (base, bits[0]))
            kept = call(
                part(body, True),
                "image_keep",
                struct((count, piece), F32),
                sides[at],
                flops // 8,
            )
            work[at] = (kept, work[at][1])
        for level in range(1, pair_size.bit_length() - 1):
            for at, (base, bits, full) in enumerate(chunks):
                if level < len(bits):
                    size = chunk_width >> (level + 1)
                    sent, kept = call(
                        part(split_body, bits[level]),
                        "split",
                        (struct((count, size), BF), struct((count, size), F32)),
                        work[at],
                    )
                    work[at] = (kept, swap(sent, "pair", bits[level]))
                else:
                    sent = call(sum_body, "sum", struct((count, shard), BF), work[at])
                    work[at] = (sent, swap(sent, "pair", full[level - len(bits)]))
        summed = degree < SUMMED
        for at, (base, bits, full) in enumerate(chunks):
            made = call(
                part(recur_body, degree == 0, at == 0 if summed else None),
                "recur",
                (
                    struct((count, shard), F32),
                    struct((count, shard), BF),
                    *[struct(sums.shape, F32)] * summed,
                ),
                (*work[at], current[at], previous[at], *((z[at], sums) if summed else ())),
            )
            new, sent = made[:2]
            sums = made[2] if summed else sums
            following.append(new)
            work[at] = (sent, [swap(sent, "pair", step) for step in steps_of(bits)])
        return following, work, sums

    for degree in range(ITERS):
        rows = later_rows(gathered) if degree else opening
        sums, args = scaled_rows(degree, sums, *rows)
        if degree < ITERS - 1:
            following, gathered, sums = next_vectors(degree, args, current, previous, sums)
            previous, current = current, following

    blocks, each = pair_size // 2, count // pair_size
    work, left_bits = [], []
    by_halves = each % 8 == 0
    for at, (side, (base, bits, full)) in enumerate(zip((left, right), chunks)):
        if by_halves:
            outs = [struct((blocks, each, chunk_width), kind) for kind in (BF, F32)]
        else:
            outs = [struct((pair_size, each, chunk_width), BF)]
        sent, *kept = call(
            part(image_last_body, base, bits, bits[0], copies),
            "image_last",
            outs,
            (side, *args, current[at], previous[at]),
            flops // 4,
            [pltpu.VMEM((count, chunk_width), F32)],
        )
        if not by_halves:
            work.append([lax.all_to_all(sent, "pair", split_axis=0, concat_axis=0)])
            continue
        work.append((kept[0], swap(sent, "pair", bits[0])))
        left_bits.append(sorted(set(bits + full) - {bits[0]}))
    while by_halves and blocks > 1:
        blocks //= 2
        for at, (base, bits, full) in enumerate(chunks):
            bit = [x for x in bits + full if x in left_bits[at]][0]
            sent, kept = call(
                part(halve_body, bit, 1 << left_bits[at].index(bit)),
                "halve",
                (struct((blocks, each, chunk_width), BF), struct((blocks, each, chunk_width), F32)),
                work[at],
            )
            left_bits[at].remove(bit)
            work[at] = (kept, swap(sent, "pair", bit))
    args = [x for pair in work for x in pair]
    last = call(last_body if by_halves else last_whole_body, "last", struct((each, width), F32), args)

    divisor = count * width * aux_size
    moments, energy = call(
        functools.partial(finish_body, divisor, cheb_coefficients(ITERS + 1)),
        "finish",
        (struct((1, ITERS + 1), F32), struct((1, 1), F32)),
        (sums, work[0][0]),
    )
    moments, energy = moments.reshape(ITERS + 1), energy.reshape(1)
    return (last.T, moments, energy)


def solution(mesh):
    placed = (P("pair", "aux"), P("pair"), P("aux", None))
    return jax.shard_map(
        per_device,
        mesh=mesh,
        in_specs=placed,
        out_specs=(P("aux", "pair"), P(), P()),
        check_vma=False,
    )
```

```python
import functools

import jax
import jax.numpy as jnp
import numpy as np
from jax import lax
from jax.experimental import pallas as pl
from jax.experimental.pallas import tpu as pltpu
from jax.sharding import PartitionSpec as P

ITERS = 8
SUMMED = ITERS // 2


spread = 5.0


BF = jnp.bfloat16
F32 = jnp.float32
VM = pl.BlockSpec(memory_space=pltpu.VMEM)
TILE = 512
PIECE = 256


def cheb_coefficients(order_count):
    node_count = 64
    angles = (np.arange(node_count) + 0.5) * np.pi / node_count
    samples = np.log(1.0 + spread * (np.cos(angles) + 1.0) / 2.0)
    values = [
        2.0 / node_count * np.sum(samples * np.cos(degree * angles))
        for degree in range(order_count)
    ]
    values[0] = values[0] / 2.0
    return np.array(values)


def call(body, name, outs, args, flops=0, scratch=(), limit=8, specs=None):
    moved = sum(a.size * a.dtype.itemsize for a in args)
    return pl.pallas_call(
        body,
        out_shape=outs,
        in_specs=specs or [VM] * len(args),
        out_specs=jax.tree.map(lambda _: VM, outs),
        scratch_shapes=scratch,
        compiler_params=pltpu.CompilerParams(vmem_limit_bytes=limit << 20),
        cost_estimate=pl.CostEstimate(flops=flops, bytes_accessed=moved, transcendentals=0),
        name=name,
    )(*args)


def struct(shape, dtype):
    return jax.ShapeDtypeStruct(shape, dtype)


def swap(x, axis, bit):
    size = lax.axis_size(axis)
    return lax.ppermute(x, axis, [(i, i ^ bit) for i in range(size)])


def bit_of(axis, bit):
    return lax.rem(lax.div(lax.axis_index(axis), jnp.int32(bit)), jnp.int32(2))


def span(start, size):
    return pl.ds(pl.multiple_of(start, size), size)


def tiles(width, tile, step, unroll=1):
    def run(k, carry):
        step(pl.multiple_of(k * tile, tile))
        return carry

    lax.fori_loop(0, width // tile, run, 0, unroll=min(unroll, width // tile))


def start_body(chunks, b, wide, w, left, right, turned_left, turned_right, give, keep, weights, sums, *refs):
    shards, (v, sems) = refs[:-2], refs[-2:]
    sums[...] = jnp.zeros_like(sums)
    pairs, width = b.shape
    half = pairs // 2
    core = bit_of("aux", 1)

    sides = ((left, turned_left, 0), (right, turned_right, left.shape[1]))

    def copy(k, side):
        held, _, base = side
        at = span(lax.rem((1 - core) * half + k * PIECE, pairs), PIECE)
        source = b.at[at, base : base + held.shape[1]]
        return pltpu.make_async_copy(source, held.at[at], sems.at[k, 0 if base == 0 else 1]), at

    for k in range(pairs // PIECE):
        for side in sides:
            copy(k, side)[0].start()
    v[...] = wide[...].astype(BF)
    weights[...] = w[:, span(core * half, half)]
    for (base, bits, _), z in zip(chunks, shards):
        z[...] = wide[:, span(shard_start(base, bits, width // len(chunks)), z.shape[1])]

    for part, out in enumerate((give, keep)):
        first = part * out.shape[1] // PIECE

        def step(n, out=out, first=first):
            k = lax.div(n, jnp.int32(PIECE))
            acc = 0.0
            for side in sides:
                move, at = copy(k + first, side)
                move.wait()
                held, turned, base = side
                for c in range(0, turned.shape[0], PIECE):
                    turned[c : c + PIECE, at] = held[at, c : c + PIECE].T
                cols = v[:, base : base + turned.shape[0]]
                acc = acc + jnp.dot(cols, turned[:, at], preferred_element_type=F32)
            out[:, pl.ds(n, PIECE)] = acc.astype(out.dtype)

        tiles(out.shape[1], PIECE, step)


def block_of(step, order):
    block = 0
    for bit in order:
        mine = bit_of("pair", bit)
        block = 2 * block + (1 - mine if step & bit else mine)
    return block


def block_span(step, order, size):
    return span(block_of(step, order) * size, size)


def steps_of(order):
    return list(range((1 << len(order)) - 1, 0, -1))


def rows_own_body(orders, left, right, own_left, own_right, o):
    tile = min(TILE, o.shape[1])
    near = [block_span(0, order, own_left.shape[1]) for order in orders]

    def step(n):
        at = pl.ds(n, tile)
        acc = jnp.dot(own_left[...], left[near[0], at], preferred_element_type=F32)
        o[:, at] = acc + jnp.dot(own_right[...], right[near[1], at], preferred_element_type=F32)

    tiles(o.shape[1], tile, step, 2)


def add_far(order, turned, far, at, acc):
    for step, block in zip(steps_of(order), far):
        side = block_span(step, order, block.shape[1])
        acc = acc + jnp.dot(block[...], turned[side, at], preferred_element_type=F32)
    return acc


def rows_far_body(order, turned, before, *refs):
    far, o = refs[:-1], refs[-1]
    tile = min(TILE, o.shape[1])

    def step(n):
        at = pl.ds(n, tile)
        o[:, at] = add_far(order, turned, far, at, before[:, at])

    tiles(o.shape[1], tile, step)


def rows_end_body(order, keep, turned, before, *refs):
    far, o = refs[:-1], refs[-1]
    tile = min(TILE, o.shape[1])
    core = bit_of("aux", 1)
    start = (core if keep else 1 - core) * o.shape[1]

    def step(n):
        at = span(start + n, tile)
        o[:, pl.ds(n, tile)] = add_far(order, turned, far, at, before[:, at]).astype(o.dtype)

    tiles(o.shape[1], tile, step, 2)


def add_body(keep, got, total, sent):
    t = keep[...] + got[...].astype(F32)
    total[...] = t
    sent[...] = t.astype(BF)


def scale_body(total, got, w, *refs):
    refs[-1][...] = (w[...] * (total[...] + got[...].astype(F32))).astype(BF)


def image_first_body(left, right, own, o):
    width, half = left.shape[1], own.shape[1]
    at = span(bit_of("aux", 1) * half, half)

    def step(n):
        for b, base in ((left, 0), (right, width)):
            acc = jnp.dot(own[...], b[at, pl.ds(n, TILE)], preferred_element_type=F32)
            o[:, pl.ds(pl.multiple_of(base + n, TILE), TILE)] = acc

    tiles(width, TILE, step, 2)


def image_dot(b, far, cols):
    half = far.shape[1]
    at = span((1 - bit_of("aux", 1)) * half, half)
    return jnp.dot(far[...], b[at, cols], preferred_element_type=F32)


def image_second_body(region, keep, b, far, first, o):
    base, bit = region
    width = o.shape[1]
    tile = min(TILE, width)
    mine = bit_of("pair", bit)
    part = mine if keep else 1 - mine

    def step(n):
        acc = image_dot(b, far, span(part * width + n, tile))
        acc = first[:, span(base + part * width + n, tile)] + acc
        o[:, pl.ds(n, tile)] = acc.astype(o.dtype)

    tiles(width, tile, step, 1 if keep else 2)


def split_body(bit, keep, got, sent, kept):
    width = kept.shape[1]
    mine = bit_of("pair", bit)
    stay, leave = span(mine * width, width), span((1 - mine) * width, width)
    sent[...] = (keep[:, leave] + got[:, leave].astype(F32)).astype(BF)
    kept[...] = keep[:, stay] + got[:, stay].astype(F32)


def sum_body(keep, got, sent):
    sent[...] = (keep[...].astype(F32) + got[...].astype(F32)).astype(BF)


def shard_start(base, bits, width):
    start = base
    for bit in bits:
        width //= 2
        start = start + bit_of("pair", bit) * width
    return start


def picked(k, bit, value):
    return k // bit * 2 * bit + k % bit + value * bit


def image_last_body(base, bits, bit, copies, b, far, first, cur, prev, *refs):
    outs, whole = refs[:-1], refs[-1]
    width = b.shape[1]
    blocks, count, _ = outs[0].shape

    def step(n):
        cols = pl.ds(pl.multiple_of(base + n, TILE), TILE)
        acc = first[:, cols] + image_dot(b, far, pl.ds(n, TILE))
        whole[:, pl.ds(n, TILE)] = (4.0 / spread) * acc

    tiles(width, TILE, step, 2)
    cols = span(shard_start(0, bits, width), cur.shape[1])
    whole[:, cols] = whole[:, cols] - (2.0 / copies) * cur[...] - (1.0 / copies) * prev[...]
    if len(outs) == 1:
        for k in range(blocks):
            outs[0][k] = whole[k * count : (k + 1) * count, :].astype(BF)
        return
    sent, kept = outs
    mine = bit_of("pair", bit)
    for k in range(blocks):
        sent[k] = whole[span(picked(k, bit, 1 - mine) * count, count), :].astype(BF)
        kept[k] = whole[span(picked(k, bit, mine) * count, count), :]


def halve_body(bit, at, keep, got, sent, kept):
    mine = bit_of("pair", bit)
    for k in range(kept.shape[0]):
        leave, stay = picked(k, at, 1 - mine), picked(k, at, mine)
        sent[k] = (keep[leave] + got[leave].astype(F32)).astype(BF)
        kept[k] = keep[stay] + got[stay].astype(F32)


def last_whole_body(*refs):
    ins, o = refs[:-1], refs[-1]
    width = o.shape[1] // len(ins)
    for k, got in enumerate(ins):
        total = got[0].astype(F32)
        for p in range(1, got.shape[0]):
            total = total + got[p].astype(F32)
        o[:, k * width : (k + 1) * width] = total


def last_body(*refs):
    ins, o = refs[:-1], refs[-1]
    width = o.shape[1] // (len(ins) // 2)
    for k in range(len(ins) // 2):
        cols = slice(k * width, (k + 1) * width)
        o[:, cols] = ins[2 * k][0] + ins[2 * k + 1][0].astype(F32)


def lane_sums(x):
    rows = jnp.sum(x, axis=0, keepdims=True)
    out = rows[:, :128]
    for n in range(128, rows.shape[1], 128):
        out = out + rows[:, n : n + 128]
    return out


def recur_body(opening, push, mine, got, cur, prev, *refs):
    image = mine[...].astype(F32) + got[...].astype(F32)
    mapped = (2.0 / spread) * image - cur[...]
    value = mapped if opening else 2.0 * mapped - prev[...]
    if push is None:
        new, sent = refs
    else:
        z, sums_in, new, sent, sums = refs
    new[...] = value
    sent[...] = value.astype(BF)
    if push is None:
        return
    before = z[...] if opening else value
    rows = [z[...] * value, before * cur[...], value * value]
    if push:
        sums[3:] = sums_in[:-3]
    else:
        sums[...] = sums_in[...]
    for k, row in enumerate(rows):
        total = lane_sums(row)
        sums[k : k + 1] = total if push else sums_in[k : k + 1] + total


def tie_body(x, after, o):
    o[...] = x[...]


def finish_body(divisor, coefficients, sums, after, moments, energy):
    totals = jnp.sum(sums[...], axis=1, keepdims=True) / divisor

    def total(order, k):
        row = 3 * (SUMMED - order) + k
        return totals[row : row + 1]

    found = [total(1, 1)] + [total(order, 0) for order in range(1, SUMMED + 1)]
    found += [2.0 * total(order // 2 + order % 2, 2 - order % 2) - found[order % 2] for order in range(SUMMED + 1, ITERS + 1)]
    lane = lax.broadcasted_iota(jnp.int32, moments.shape, 1)
    row = jnp.zeros(moments.shape, F32)
    weighed = jnp.zeros(energy.shape, F32)
    for k, coefficient in enumerate(coefficients):
        row = jnp.where(lane == k, found[k], row)
        weighed = weighed + float(coefficient) * found[k]
    moments[...] = row
    energy[...] = weighed


def per_device(pair_factors, pair_weights, probes):
    aux_size, pair_size = lax.axis_size("aux"), lax.axis_size("pair")
    pairs, width = pair_factors.shape
    count = probes.shape[1]
    half = pairs // 2
    flops = 2 * pairs * width * count
    part = functools.partial

    order = [1 << k for k in range(pair_size.bit_length() - 1)]
    lower, beyond = order[:2], order[2:]
    chunk_width = width // 2
    chunks = [(0, lower[::-1], beyond), (chunk_width, lower, beyond)]
    copies = 1 << len(beyond)
    shard = chunk_width * copies // pair_size

    left, right, turned_left, turned_right, *opening, weights, sums, z_left, z_right = call(
        part(start_body, chunks),
        "start",
        (
            pltpu.VMEM((pairs, chunk_width), BF),
            pltpu.VMEM((pairs, chunk_width), BF),
            pltpu.VMEM((chunk_width, pairs), BF),
            pltpu.VMEM((chunk_width, pairs), BF),
            struct((count, half), BF),
            struct((count, half), F32),
            struct((1, half), F32),
            struct((16, 128), F32),
            *[struct((count, shard), F32) for _ in chunks],
        ),
        (pair_factors, probes.T, pair_weights[None, :]),
        flops,
        [pltpu.VMEM((count, width), BF), pltpu.SemaphoreType.DMA((pairs // PIECE, 2))],
        20,
        [pl.BlockSpec(memory_space=pltpu.HBM), VM, VM],
    )
    z = [z_left, z_right]
    previous, current = list(z), list(z)
    hops = [("aux", 1 << k) for k in range(aux_size.bit_length() - 1)]
    hops += [("pair", bit) for bit in lower]
    late = ITERS - SUMMED
    rounds = [hops[k - SUMMED :: late] if k >= SUMMED else [] for k in range(ITERS)]
    outs = (struct((count, half), F32), struct((count, half), BF))

    def later_rows(gathered):
        (own_left, far_left), (own_right, far_right) = gathered
        whole = struct((count, pairs), F32)
        orders = [bits for _, bits, _ in chunks]
        rows = call(
            part(rows_own_body, orders),
            "rows_own",
            whole,
            (turned_left, turned_right, own_left, own_right),
            flops // 4,
        )
        rows = call(
            part(rows_far_body, orders[0]),
            "rows_far",
            whole,
            (turned_left, rows, *far_left),
            flops // 3,
        )
        args = (turned_right, rows, *far_right)
        return [
            call(
                part(rows_end_body, orders[1], keep),
                "rows_keep" if keep else "rows_give",
                struct((count, half), F32 if keep else BF),
                args,
                flops // 8,
            )
            for keep in (False, True)
        ]

    def scaled_rows(degree, sums, give, total):
        got = swap(give, "aux", 1)
        bit = 2
        while bit < aux_size:
            total, sent = call(add_body, "add", outs, (total, got))
            got = swap(sent, "aux", bit)
            bit *= 2
        for axis, bit in rounds[degree]:
            tied = call(tie_body, "tie", struct(sums.shape, F32), (sums, sent))
            sums = tied + swap(tied, axis, bit)
        order = [sums] * bool(rounds[degree])
        own = call(scale_body, "scale", struct((count, half), BF), (total, got, weights, *order))
        far = swap(own, "aux", 1)
        whole = struct((count, width), F32)
        image = call(image_first_body, "image_first", whole, (left, right, own), flops // 2)
        return sums, (far, image)

    piece = chunk_width // 2

    def next_vectors(degree, args, current, previous, sums):
        work, following = [], []
        sides = ((left, *args), (right, *args))
        for side, (base, bits, full) in zip(sides, chunks):
            body = part(image_second_body, (base, bits[0]))
            sent = call(
                part(body, False), "image_give", struct((count, piece), BF), side, flops // 8
            )
            got = swap(sent, "pair", bits[0])
            work.append((sent, got))
        for at, (base, bits, full) in enumerate(chunks):
            body = part(image_second_body, (base, bits[0]))
            kept = call(
                part(body, True),
                "image_keep",
                struct((count, piece), F32),
                sides[at],
                flops // 8,
            )
            work[at] = (kept, work[at][1])
        for level in range(1, pair_size.bit_length() - 1):
            for at, (base, bits, full) in enumerate(chunks):
                if level < len(bits):
                    size = chunk_width >> (level + 1)
                    sent, kept = call(
                        part(split_body, bits[level]),
                        "split",
                        (struct((count, size), BF), struct((count, size), F32)),
                        work[at],
                    )
                    work[at] = (kept, swap(sent, "pair", bits[level]))
                else:
                    sent = call(sum_body, "sum", struct((count, shard), BF), work[at])
                    work[at] = (sent, swap(sent, "pair", full[level - len(bits)]))
        summed = degree < SUMMED
        for at, (base, bits, full) in enumerate(chunks):
            made = call(
                part(recur_body, degree == 0, at == 0 if summed else None),
                "recur",
                (
                    struct((count, shard), F32),
                    struct((count, shard), BF),
                    *[struct(sums.shape, F32)] * summed,
                ),
                (*work[at], current[at], previous[at], *((z[at], sums) if summed else ())),
            )
            new, sent = made[:2]
            sums = made[2] if summed else sums
            following.append(new)
            work[at] = (sent, [swap(sent, "pair", step) for step in steps_of(bits)])
        return following, work, sums

    for degree in range(ITERS):
        rows = later_rows(gathered) if degree else opening
        sums, args = scaled_rows(degree, sums, *rows)
        if degree < ITERS - 1:
            following, gathered, sums = next_vectors(degree, args, current, previous, sums)
            previous, current = current, following

    blocks, each = pair_size // 2, count // pair_size
    work, left_bits = [], []
    by_halves = each % 8 == 0
    for at, (side, (base, bits, full)) in enumerate(zip((left, right), chunks)):
        if by_halves:
            outs = [struct((blocks, each, chunk_width), kind) for kind in (BF, F32)]
        else:
            outs = [struct((pair_size, each, chunk_width), BF)]
        sent, *kept = call(
            part(image_last_body, base, bits, bits[0], copies),
            "image_last",
            outs,
            (side, *args, current[at], previous[at]),
            flops // 4,
            [pltpu.VMEM((count, chunk_width), F32)],
        )
        if not by_halves:
            work.append([lax.all_to_all(sent, "pair", split_axis=0, concat_axis=0)])
            continue
        work.append((kept[0], swap(sent, "pair", bits[0])))
        left_bits.append(sorted(set(bits + full) - {bits[0]}))
    while by_halves and blocks > 1:
        blocks //= 2
        for at, (base, bits, full) in enumerate(chunks):
            bit = [x for x in bits + full if x in left_bits[at]][0]
            sent, kept = call(
                part(halve_body, bit, 1 << left_bits[at].index(bit)),
                "halve",
                (struct((blocks, each, chunk_width), BF), struct((blocks, each, chunk_width), F32)),
                work[at],
            )
            left_bits[at].remove(bit)
            work[at] = (kept, swap(sent, "pair", bit))
    args = [x for pair in work for x in pair]
    last = call(last_body if by_halves else last_whole_body, "last", struct((each, width), F32), args)

    divisor = count * width * aux_size
    moments, energy = call(
        functools.partial(finish_body, divisor, cheb_coefficients(ITERS + 1)),
        "finish",
        (struct((1, ITERS + 1), F32), struct((1, 1), F32)),
        (sums, work[0][0]),
    )
    moments, energy = moments.reshape(ITERS + 1), energy.reshape(1)
    return (last.T, moments, energy)


def solution(mesh):
    placed = (P("pair", "aux"), P("pair"), P("aux", None))
    return jax.shard_map(
        per_device,
        mesh=mesh,
        in_specs=placed,
        out_specs=(P("aux", "pair"), P(), P()),
        check_vma=False,
    )
```
